32 devices in a mesh: seq: 8 (over z, x), chan: 4 (over y, core).
Axes of the slice: x: 2, y: 2, z: 4, core: 2. Of those that a mesh axis runs over, the one named last changes fastest.
Arguments:
- inputs: bfloat16 [2048, 2048], P('seq', 'chan'), may hold values from -6 to 6
- weights: bfloat16 [4, 2048, 2048], P(None, None, 'chan'), may hold values from -0.125 to 0.125
- filters: float32 [4, 2048], P(None, 'seq'), may hold values from -0.125 to 0.125
Outputs:
- output: bfloat16 [2048, 2048], P('seq', 'chan')
The draws below stay inside these ranges and needn't reach their ends.
All inputs are finite; a program needn't handle non-finite values.
Results may differ from the reference program's by a relative error of at most 0.0049.
Values may be sent and summed in bfloat16 or wider, within the bound.
No kernel may reach another device: no remote copies, remote signals or barrier semaphores. Data moves between devices by JAX's collectives and lax.ppermute only.
A program may use at most 64 MiB of HBM per device.

```python
import jax
import jax.numpy as jnp
from jax import lax

D = 2048
K = 4
L = 2048


def steps_of(rng, shape, pieces, low, top_value):
    gain, own = 1.0, jax.random.fold_in(rng, 6)
    for axis_at, shards_of in pieces:
        steps = jnp.exp(jax.random.uniform(jax.random.fold_in(own, axis_at), (shards_of,), jnp.float32, low / len(pieces), top_value / len(pieces)))
        gain = gain * jnp.repeat(steps, shape[axis_at] // shards_of).reshape([-1 if axis == axis_at else 1 for axis in range(len(shape))])
    return gain


def noise(key, extent, spread, most, split=(), held_as=jnp.bfloat16):
    drawn = spread * jax.random.normal(key, extent, jnp.float32)
    if split:
        drawn = drawn * steps_of(key, extent, split, -0.22, 0.18)
    return jnp.clip(drawn, -most, most).astype(held_as)


def setup_inputs(seed: int = 0) -> dict:
    key_list = jax.random.split(jax.random.key(seed), 4)
    inputs = noise(key_list[0], (L, D), 1.0, 6.0, ((0, 8), (1, 4)))
    weights = noise(key_list[1], (K, D, D), D ** -0.5, 0.125, ((2, 4),))
    filters = noise(key_list[2], (K, L), L ** -0.5, 0.125, ((1, 8),), jnp.float32)
    return dict(inputs=inputs, weights=weights, filters=filters)


def reference(inputs, weights, filters):
    length = inputs.shape[0]
    total = 2 * length

    def add_filter(summed, pair):
        weight, filter_row = pair
        projected = jnp.dot(inputs, weight, preferred_element_type=jnp.float32).astype(jnp.bfloat16)
        projected = lax.optimization_barrier(projected).astype(jnp.float32)
        spectrum = jnp.fft.rfft(projected, n=total, axis=0) * jnp.fft.rfft(filter_row, n=total)[:, None]
        convolved = jnp.fft.irfft(spectrum, n=total, axis=0)[:length]
        return summed + convolved.astype(summed.dtype), None

    start = jnp.zeros(inputs.shape, jnp.float32)
    summed, unused = lax.scan(add_filter, start, (weights, filters))
    return summed.astype(jnp.bfloat16)
```

```python
import functools
import math

import jax
import jax.numpy as jnp
from jax import lax
from jax.experimental import pallas as pl
from jax.experimental.pallas import tpu as pltpu
from jax.sharding import PartitionSpec as P

f32 = jnp.float32
bf16 = jnp.bfloat16
LANES = 128


def swap(value, axis, mask):
    return lax.ppermute(value, axis, [(i, i ^ mask) for i in range(lax.axis_size(axis))])


def params(mib, axes=1):
    return pltpu.CompilerParams(
        dimension_semantics=("arbitrary",) * axes, vmem_limit_bytes=mib * 1024 * 1024
    )


def project_body(meta, *refs, steps, group, has_sum, last):
    x_refs, w_ref = refs[:steps], refs[steps]
    refs = refs[steps + 1 :]
    if has_sum:
        sum_ref, refs = refs[0], refs[1:]
    count = group if last else 1
    out_refs, (held, total) = refs[:count], refs[count:]
    step, k = pl.program_id(0), pl.program_id(1)
    filters = pl.num_programs(1)
    width = w_ref.shape[2]
    sub = width // group
    place = meta[1]

    @pl.when((step == 0) & (k == 0))
    def _():
        for at, x_ref in enumerate(x_refs):
            held[at] = x_ref[...]

    columns = [
        w_ref[0, :, pl.ds(pl.multiple_of((place ^ m) * sub, sub), sub)] for m in range(group)
    ]
    part = jnp.dot(held[step], jnp.concatenate(columns, axis=1), preferred_element_type=f32)
    if has_sum:
        before = jnp.where(step == 0, sum_ref[0], total[k])
        part = part + before
    else:
        part = jnp.where(step == 0, part, part + total[k])
    total[k] = part

    @pl.when((step == steps - 1) & (k == filters - 1))
    def _():
        for j in range(total.shape[0]):
            if last:
                for m in range(group):
                    out_refs[m][:, j * sub : (j + 1) * sub] = total[
                        j, :, m * sub : (m + 1) * sub
                    ].astype(bf16)
            else:
                out_refs[0][j] = total[j]


def project(meta, order, blocks, weights, before, group, last):
    steps = len(blocks)
    tokens, depth = blocks[0].shape
    count, _, width = weights.shape
    whole = pl.BlockSpec((tokens, depth), lambda i, k, meta: (0, 0))
    first, mask = order[0], order[0] ^ order[-1]

    def w_map(i, k, meta):
        return (k, meta[0] ^ (first ^ (i * mask)), 0)

    in_specs = [whole] * steps + [pl.BlockSpec((1, depth, width), w_map)]
    args = [*blocks, weights]
    if before is not None:
        in_specs.append(
            pl.BlockSpec((1, tokens, width), lambda i, k, meta: (jnp.where(i == 0, k, count - 1), 0, 0))
        )
        args.append(before)
    if last:
        shape = (tokens, count * width // group)
        out_shape = [jax.ShapeDtypeStruct(shape, bf16)] * group
        out_specs = [pl.BlockSpec(shape, lambda i, k, meta: (0, 0))] * group
    else:
        shape = (count, tokens, width)
        out_shape = [jax.ShapeDtypeStruct(shape, f32)]
        out_specs = [pl.BlockSpec(shape, lambda i, k, meta: (0, 0, 0))]
    return pl.pallas_call(
        functools.partial(
            project_body, steps=steps, group=group, has_sum=before is not None, last=last
        ),
        grid_spec=pltpu.PrefetchScalarGridSpec(
            num_scalar_prefetch=1,
            grid=(steps, count),
            in_specs=in_specs,
            out_specs=out_specs,
            scratch_shapes=[
                pltpu.VMEM((steps, tokens, depth), bf16),
                pltpu.VMEM((count, tokens, width), f32),
            ],
        ),
        out_shape=out_shape,
        compiler_params=params(24, 2),
        cost_estimate=pl.CostEstimate(
            flops=2 * steps * tokens * depth * width * count,
            bytes_accessed=2 * steps * depth * width * count,
            transcendentals=0,
        ),
        name="project_last" if last else "project_first",
    )(meta, *args)


def toeplitz_body(meta, pieces_ref, out_ref, row, *, order, group):
    count, width = pieces_ref.shape[1:]
    length = len(order) * width
    step = pl.program_id(0)

    @pl.when(step == 0)
    def _():
        row[:, pl.ds(length, width)] = jnp.zeros((row.shape[0], width), f32)
        for at, m in enumerate(order):
            start = length - width * ((meta[3] ^ m) + 1)
            row[0:count, pl.ds(pl.multiple_of(start, width), width)] = pieces_ref[at]

    span = group * width
    start = pl.multiple_of(length - span * (step + 1), width)
    for k in range(count):
        line = jnp.broadcast_to(row[k : k + 1, pl.ds(start, span + width)], (LANES, span + width))
        turned = pltpu.roll(line, 1, 1, stride=1, stride_axis=0).astype(bf16)
        for e in range(group):
            for h in range(width // LANES):
                at = span - width * e - LANES * h
                out_ref[
                    e * width + h * LANES : e * width + (h + 1) * LANES, k * width : (k + 1) * width
                ] = turned[:, at : at + width]


def toeplitz(meta, pieces, order, group):
    blocks, count, width = pieces.shape
    rows, columns = group * width, count * width
    return pl.pallas_call(
        functools.partial(toeplitz_body, order=order, group=group),
        grid_spec=pltpu.PrefetchScalarGridSpec(
            num_scalar_prefetch=1,
            grid=(blocks // group,),
            in_specs=[pl.BlockSpec(pieces.shape, lambda i, meta: (0, 0, 0))],
            out_specs=pl.BlockSpec((rows, columns), lambda i, meta: (i, 0)),
            scratch_shapes=[pltpu.VMEM((8, (blocks + 1) * width), f32)],
        ),
        out_shape=jax.ShapeDtypeStruct((blocks * width, columns), bf16),
        compiler_params=params(16),
        cost_estimate=pl.CostEstimate(
            flops=blocks * width * columns * 8,
            bytes_accessed=2 * blocks * width * columns,
            transcendentals=0,
        ),
        name="toeplitz",
    )(meta, pieces)


def convolve_body(meta, *refs, group, sub, own):
    if own:
        low_ref, high_ref, refs = None, refs[0], refs[1:]
    else:
        low_ref, high_ref, refs = refs[0], refs[1], refs[2:]
    p_refs, out_refs, (held, placed) = refs[:group], refs[group : 2 * group], refs[2 * group :]
    width = p_refs[0].shape[0]
    count = p_refs[0].shape[1] // sub
    place = meta[1]

    @pl.when(pl.program_id(0) == 0)
    def _():
        for m, p_ref in enumerate(p_refs):
            at = pl.multiple_of((place ^ m) * sub, sub)
            for k in range(count):
                held[k * width : (k + 1) * width, pl.ds(at, sub)] = p_ref[
                    :, k * sub : (k + 1) * sub
                ]

    sums = [None] * group
    for pair in range(0, group, 2):
        side = held[:, pair * sub : (pair + 2) * sub]
        top = group - pair
        high = jnp.dot(high_ref[0 : top * width, :], side, preferred_element_type=f32)
        if not own:
            least = group - pair - 1
            low = jnp.dot(low_ref[least * width :, :], side, preferred_element_type=f32)
        for b in (pair, pair + 1):
            lanes = slice((b - pair) * sub, (b - pair + 1) * sub)
            for r in range(group):
                e = r - b
                if e >= 0:
                    term = high[e * width : (e + 1) * width, lanes]
                elif own:
                    continue
                else:
                    e += group - least
                    term = low[e * width : (e + 1) * width, lanes]
                sums[r] = term if sums[r] is None else sums[r] + term
    for r in range(group):
        placed[place ^ r] = sums[r].astype(bf16)
    for m in range(group):
        out_refs[m][...] = placed[m]


def convolve(meta, table, parts, group, own):
    width = parts[0].shape[0]
    blocks = table.shape[0] // width
    count = table.shape[1] // width
    sub = parts[0].shape[1] // count
    rows, columns = group * width, table.shape[1]
    steps = 1 if own else blocks // group - 1
    high = pl.BlockSpec((rows, columns), lambda i, meta: (i if own else i + 1, 0))
    low = pl.BlockSpec((rows, columns), lambda i, meta: (i, 0))
    part = pl.BlockSpec(parts[0].shape, lambda i, meta: (0, 0))
    tables = [high] if own else [low, high]
    return pl.pallas_call(
        functools.partial(convolve_body, group=group, sub=sub, own=own),
        grid_spec=pltpu.PrefetchScalarGridSpec(
            num_scalar_prefetch=1,
            grid=(steps,),
            in_specs=tables + [part] * group,
            out_specs=[pl.BlockSpec((width, sub), lambda i, meta: (i, 0))] * group,
            scratch_shapes=[
                pltpu.VMEM((columns, group * sub), bf16),
                pltpu.VMEM((group, width, sub), bf16),
            ],
        ),
        out_shape=[jax.ShapeDtypeStruct((steps * width, sub), bf16)] * group,
        compiler_params=params(32),
        cost_estimate=pl.CostEstimate(
            flops=2 * steps * rows * columns * group * sub,
            bytes_accessed=2 * (steps + 1) * rows * columns,
            transcendentals=0,
        ),
        name="convolve_own" if own else "convolve_after",
    )(meta, *[table] * len(tables), *parts)


def finish_body(meta, *refs, group):
    parts, out_ref = refs[:-1], refs[-1]
    sub = out_ref.shape[1] // group
    place, own = meta[1], meta[2]
    for m in range(group):
        value = parts[m][...].astype(f32)
        for far in range(1, len(parts) // group):
            other = parts[far * group + m][...].astype(f32)
            value = value + jnp.where((own ^ far) < own, other, 0.0)
        at = pl.multiple_of((place ^ m) * sub, sub)
        out_ref[:, pl.ds(at, sub)] = value.astype(bf16)


def finish(meta, parts, group):
    width, sub = parts[0].shape
    shape = (width, sub * group)
    return pl.pallas_call(
        functools.partial(finish_body, group=group),
        grid_spec=pltpu.PrefetchScalarGridSpec(
            num_scalar_prefetch=1,
            grid=(1,),
            in_specs=[pl.BlockSpec((width, sub), lambda i, meta: (0, 0))] * len(parts),
            out_specs=pl.BlockSpec(shape, lambda i, meta: (0, 0)),
        ),
        out_shape=jax.ShapeDtypeStruct(shape, bf16),
        compiler_params=params(24),
        name="finish",
    )(meta, *parts)


def local(inputs, weights, filters):
    seq, chan = lax.axis_size("seq"), lax.axis_size("chan")
    group = min(4, seq)
    groups = seq // group
    width = inputs.shape[0]
    at_seq, at_chan = lax.axis_index("seq"), lax.axis_index("chan")
    lane = jnp.arange(4)
    meta = jnp.where(
        lane == 0,
        at_chan,
        jnp.where(lane == 1, at_seq % group, jnp.where(lane == 2, at_seq // group, at_seq)),
    ).astype(jnp.int32)

    held = {0: inputs}
    for m in range(1, chan):
        low = m & -m
        held[m] = swap(held[m - low], "chan", low)

    pieces = jnp.flip(filters, axis=1)[None]
    order = [0]
    bit = seq // 2
    while bit:
        pieces = jnp.concatenate([pieces, swap(pieces, "seq", bit)])
        order += [m ^ bit for m in order]
        bit //= 2
    table = toeplitz(meta, pieces, order, group)

    near = [m for m in range(chan) if m < 2]
    far = [m for m in range(chan) if m >= 2]
    (before,) = project(meta, near, [held[m] for m in near], weights, None, group, False)
    mine = project(meta, far, [held[m] for m in far], weights, before, group, True)
    parts = [mine[0]] + [swap(mine[m], "seq", m) for m in range(1, group)]

    pieces = []
    if groups > 1:
        after = convolve(meta, table, parts, group, False)
        for far in range(1, groups):
            ahead = jnp.maximum(((at_seq // group) ^ far) - at_seq // group - 1, 0)
            for m in range(group):
                piece = after[m]
                if groups > 2:
                    piece = lax.dynamic_slice_in_dim(piece, ahead * width, width, 0)
                pieces.append(swap(piece, "seq", far * group + m))
    own = convolve(meta, table, parts, group, True)
    pieces = [own[0]] + [swap(own[m], "seq", m) for m in range(1, group)] + pieces
    return finish(meta, pieces, group)


def solution(mesh):
    in_specs = (P("seq", "chan"), P(None, None, "chan"), P(None, "seq"))
    out_specs = P("seq", "chan")
    return jax.shard_map(local, mesh=mesh, in_specs=in_specs, out_specs=out_specs, check_vma=False)
```

```python
import functools

import jax
import jax.numpy as jnp
from jax import lax
from jax.experimental import pallas as pl
from jax.experimental.pallas import tpu as pltpu
from jax.sharding import PartitionSpec as P


f32 = jnp.float32
bf16 = jnp.bfloat16
LANES = 128


def swap(value, axis, mask):
    return lax.ppermute(value, axis, [(i, i ^ mask) for i in range(lax.axis_size(axis))])


def params(mib, axes=1):
    return pltpu.CompilerParams(
        dimension_semantics=("arbitrary",) * axes if axes else None,
        vmem_limit_bytes=mib * 1024 * 1024,
    )


def columns_of(w, place, group):
    sub = w.shape[1] // group
    return jnp.concatenate(
        [w[:, pl.ds(pl.multiple_of((place ^ m) * sub, sub), sub)] for m in range(group)], axis=1
    )


def project_first_body(meta, *refs, near, far, group):
    x_refs, w_ref = refs[: len(near)], refs[len(near)]
    sum_ref, ahead_ref, held, sems = refs[len(near) + 1 :]
    depth = x_refs[0].shape[1]
    count = w_ref.shape[0]

    def fetch(k, m, target, sem):
        rows = pl.ds(pl.multiple_of((meta[0] ^ m) * depth, depth), depth)
        return pltpu.make_async_copy(w_ref.at[k, rows, :], target, sem)

    first = [
        [fetch(k, m, held.at[k, pl.ds(j * depth, depth), :], sems.at[k, j]) for j, m in enumerate(near)]
        for k in range(count)
    ]
    later = [
        fetch(k, m, ahead_ref.at[j, k], sems.at[k, len(near) + j])
        for j, m in enumerate(far)
        for k in range(count)
    ]
    for copy in [copy for copies in first for copy in copies] + later:
        copy.start()
    x = jnp.concatenate([x_ref[...] for x_ref in x_refs], axis=1)
    for k in range(count):
        for copy in first[k]:
            copy.wait()
        sum_ref[k] = jnp.dot(x, columns_of(held.at[k], meta[1], group), preferred_element_type=f32)
    for copy in later:
        copy.wait()


def project_first(meta, near, far, blocks, weights, group):
    tokens, depth = blocks[0].shape
    count, _, width = weights.shape
    vmem = pl.BlockSpec(memory_space=pltpu.VMEM)
    return pl.pallas_call(
        functools.partial(project_first_body, near=near, far=far, group=group),
        in_specs=[pl.BlockSpec(memory_space=pltpu.SMEM)]
        + [vmem] * len(near)
        + [pl.BlockSpec(memory_space=pltpu.HBM)],
        out_specs=[vmem, vmem],
        scratch_shapes=[
            pltpu.VMEM((count, len(near) * depth, width), bf16),
            pltpu.SemaphoreType.DMA((count, len(near) + len(far))),
        ],
        out_shape=[
            jax.ShapeDtypeStruct((count, tokens, width), f32),
            jax.ShapeDtypeStruct((len(far), count, depth, width), bf16),
        ],
        compiler_params=params(32, 0),
        cost_estimate=pl.CostEstimate(
            flops=2 * len(near) * tokens * depth * width * count,
            bytes_accessed=2 * weights.size,
            transcendentals=0,
        ),
        name="project_first",
    )(meta, *blocks, weights)


def project_next_body(meta, x_ref, w_ref, sum_ref, *out_refs, at, group, last):
    count, _, width = sum_ref.shape
    sub = width // group
    for k in range(count):
        total = sum_ref[k] + jnp.dot(
            x_ref[...], columns_of(w_ref.at[at, k], meta[1], group), preferred_element_type=f32
        )
        if last:
            for m in range(group):
                out_refs[m][:, k * sub : (k + 1) * sub] = total[
                    :, m * sub : (m + 1) * sub
                ].astype(bf16)
        else:
            out_refs[0][k] = total


def project_next(meta, at, block, ahead, before, group, last):
    count, tokens, width = before.shape
    vmem = pl.BlockSpec(memory_space=pltpu.VMEM)
    if last:
        shape = (tokens, count * width // group)
        out_shape = [jax.ShapeDtypeStruct(shape, bf16)] * group
    else:
        out_shape = [jax.ShapeDtypeStruct(before.shape, f32)]
    return pl.pallas_call(
        functools.partial(project_next_body, at=at, group=group, last=last),
        in_specs=[pl.BlockSpec(memory_space=pltpu.SMEM)] + [vmem] * 3,
        out_specs=[vmem] * len(out_shape),
        out_shape=out_shape,
        compiler_params=params(32, 0),
        cost_estimate=pl.CostEstimate(
            flops=2 * tokens * block.shape[1] * width * count,
            bytes_accessed=2 * block.shape[1] * width * count,
            transcendentals=0,
        ),
        name="project_last" if last else "project_more",
    )(meta, block, ahead, before)


def toeplitz_body(meta, pieces_ref, out_ref, row, *, order, group):
    count, width = pieces_ref.shape[1:]
    length = len(order) * width
    step = pl.program_id(0)

    @pl.when(step == 0)
    def _():
        row[:, pl.ds(length, width)] = jnp.zeros((row.shape[0], width), f32)
        across = lax.broadcasted_iota(jnp.int32, (width, width), 0)
        along = lax.broadcasted_iota(jnp.int32, (width, width), 1)
        mirror = (across + along == width - 1).astype(bf16)
        turned = jnp.dot(
            pieces_ref[...].reshape(len(order) * count, width).astype(bf16),
            mirror,
            preferred_element_type=f32,
        )
        for at, m in enumerate(order):
            start = length - width * ((meta[3] ^ m) + 1)
            row[0:count, pl.ds(pl.multiple_of(start, width), width)] = turned[
                at * count : (at + 1) * count
            ]

    span = group * width
    start = pl.multiple_of(length - span * (step + 1), width)
    for k in range(count):
        line = jnp.broadcast_to(row[k : k + 1, pl.ds(start, span + width)], (LANES, span + width))
        turned = pltpu.roll(line, 1, 1, stride=1, stride_axis=0).astype(bf16)
        for e in range(group):
            for h in range(width // LANES):
                at = span - width * e - LANES * h
                out_ref[
                    e * width + h * LANES : e * width + (h + 1) * LANES, k * width : (k + 1) * width
                ] = turned[:, at : at + width]


def toeplitz(meta, pieces, order, group):
    blocks, count, width = pieces.shape
    rows, columns = group * width, count * width
    return pl.pallas_call(
        functools.partial(toeplitz_body, order=order, group=group),
        grid_spec=pltpu.PrefetchScalarGridSpec(
            num_scalar_prefetch=1,
            grid=(blocks // group,),
            in_specs=[pl.BlockSpec(pieces.shape, lambda i, meta: (0, 0, 0))],
            out_specs=pl.BlockSpec((rows, columns), lambda i, meta: (i, 0)),
            scratch_shapes=[pltpu.VMEM((8, (blocks + 1) * width), f32)],
        ),
        out_shape=jax.ShapeDtypeStruct((blocks * width, columns), bf16),
        compiler_params=params(16),
        cost_estimate=pl.CostEstimate(
            flops=blocks * width * columns * 8,
            bytes_accessed=2 * blocks * width * columns,
            transcendentals=0,
        ),
        name="toeplitz",
    )(meta, pieces)


def convolve_body(meta, *refs, group, sub, own, whole):
    if whole:
        rows = group * refs[1].shape[0]
        low_ref, high_ref, refs = refs[0].at[0:rows], refs[0].at[0 if own else rows :], refs[1:]
    elif own:
        low_ref, high_ref, refs = None, refs[0], refs[1:]
    else:
        low_ref, high_ref, refs = refs[0], refs[1], refs[2:]
    p_refs, out_refs, (held, placed) = refs[:group], refs[group : 2 * group], refs[2 * group :]
    width = p_refs[0].shape[0]
    count = p_refs[0].shape[1] // sub
    place = meta[1]

    @pl.when(True if whole else pl.program_id(0) == 0)
    def _():
        for m, p_ref in enumerate(p_refs):
            at = pl.multiple_of((place ^ m) * sub, sub)
            for k in range(count):
                held[k * width : (k + 1) * width, pl.ds(at, sub)] = p_ref[
                    :, k * sub : (k + 1) * sub
                ]

    sums = [None] * group
    for pair in range(0, group, 2):
        side = held[:, pair * sub : (pair + 2) * sub]
        top = group - pair
        high = jnp.dot(high_ref[0 : top * width, :], side, preferred_element_type=f32)
        if not own:
            least = group - pair - 1
            low = jnp.dot(low_ref[least * width :, :], side, preferred_element_type=f32)
        for b in (pair, pair + 1):
            lanes = slice((b - pair) * sub, (b - pair + 1) * sub)
            for r in range(group):
                e = r - b
                if e >= 0:
                    term = high[e * width : (e + 1) * width, lanes]
                elif own:
                    continue
                else:
                    e += group - least
                    term = low[e * width : (e + 1) * width, lanes]
                sums[r] = term if sums[r] is None else sums[r] + term
    for r in range(group):
        placed[place ^ r] = sums[r].astype(bf16)
    for m in range(group):
        out_refs[m][...] = placed[m]


def convolve(meta, table, parts, group, own):
    width = parts[0].shape[0]
    blocks = table.shape[0] // width
    count = table.shape[1] // width
    sub = parts[0].shape[1] // count
    rows, columns = group * width, table.shape[1]
    steps = 1 if own else blocks // group - 1
    high = pl.BlockSpec((rows, columns), lambda i, meta: (i if own else i + 1, 0))
    low = pl.BlockSpec((rows, columns), lambda i, meta: (i, 0))
    part = pl.BlockSpec(parts[0].shape, lambda i, meta: (0, 0))
    tables = [high] if own else [low, high]
    scratch = [pltpu.VMEM((columns, group * sub), bf16), pltpu.VMEM((group, width, sub), bf16)]
    call = functools.partial(
        pl.pallas_call,
        out_shape=[jax.ShapeDtypeStruct((steps * width, sub), bf16)] * group,
        cost_estimate=pl.CostEstimate(
            flops=2 * steps * rows * columns * group * sub,
            bytes_accessed=2 * (steps + 1) * rows * columns,
            transcendentals=0,
        ),
        name="convolve_own" if own else "convolve_after",
    )
    if blocks == 2 * group:
        vmem = pl.BlockSpec(memory_space=pltpu.VMEM)
        return call(
            functools.partial(convolve_body, group=group, sub=sub, own=own, whole=True),
            in_specs=[pl.BlockSpec(memory_space=pltpu.SMEM)] + [vmem] * (1 + group),
            out_specs=[vmem] * group,
            scratch_shapes=scratch,
            compiler_params=params(32, 0),
        )(meta, table, *parts)
    return call(
        functools.partial(convolve_body, group=group, sub=sub, own=own, whole=False),
        grid_spec=pltpu.PrefetchScalarGridSpec(
            num_scalar_prefetch=1,
            grid=(steps,),
            in_specs=tables + [part] * group,
            out_specs=[pl.BlockSpec((width, sub), lambda i, meta: (i, 0))] * group,
            scratch_shapes=scratch,
        ),
        compiler_params=params(32),
    )(meta, *[table] * len(tables), *parts)


def finish_body(meta, *refs, group):
    parts, out_ref = refs[:-1], refs[-1]
    sub = out_ref.shape[1] // group
    place, own = meta[1], meta[2]
    for m in range(group):
        value = parts[m][...].astype(f32)
        for far in range(1, len(parts) // group):
            other = parts[far * group + m][...].astype(f32)
            value = value + jnp.where((own ^ far) < own, other, 0.0)
        at = pl.multiple_of((place ^ m) * sub, sub)
        out_ref[:, pl.ds(at, sub)] = value.astype(bf16)


def finish(meta, parts, group):
    width, sub = parts[0].shape
    shape = (width, sub * group)
    return pl.pallas_call(
        functools.partial(finish_body, group=group),
        in_specs=[pl.BlockSpec(memory_space=pltpu.SMEM)]
        + [pl.BlockSpec(memory_space=pltpu.VMEM)] * len(parts),
        out_specs=pl.BlockSpec(memory_space=pltpu.VMEM),
        out_shape=jax.ShapeDtypeStruct(shape, bf16),
        compiler_params=params(24, 0),
        name="finish",
    )(meta, *parts)


def local(inputs, weights, filters):
    seq, chan = lax.axis_size("seq"), lax.axis_size("chan")
    group = min(4, seq)
    groups = seq // group
    width = inputs.shape[0]
    at_seq, at_chan = lax.axis_index("seq"), lax.axis_index("chan")
    lane = jnp.arange(4)
    meta = jnp.where(
        lane == 0,
        at_chan,
        jnp.where(lane == 1, at_seq % group, jnp.where(lane == 2, at_seq // group, at_seq)),
    ).astype(jnp.int32)

    far = [m for m in range(chan) if m >= 2]
    held = {0: inputs}
    held[2] = swap(inputs, "chan", 2)
    held[1] = swap(inputs, "chan", 1)
    held[3] = swap(held[2], "chan", 1)

    pieces = filters[None]
    order = [0]
    bit = seq // 2
    while bit:
        pieces = jnp.concatenate([pieces, swap(pieces, "seq", bit)])
        order += [m ^ bit for m in order]
        bit //= 2
    table = toeplitz(meta, pieces, order, group)

    before, ahead = project_first(meta, [0, 1], far, [held[0], held[1]], weights, group)
    (before,) = project_next(meta, 0, held[2], ahead, before, group, False)
    mine = project_next(meta, 1, held[3], ahead, before, group, True)
    parts = {0: mine[0]}
    for m in reversed(range(1, group)):
        parts[m] = swap(mine[m], "seq", m)
    parts = [parts[m] for m in range(group)]

    pieces = []
    if groups > 1:
        after = convolve(meta, table, parts, group, False)
        for far in range(1, groups):
            ahead = jnp.maximum(((at_seq // group) ^ far) - at_seq // group - 1, 0)
            for m in range(group):
                piece = after[m]
                if groups > 2:
                    piece = lax.dynamic_slice_in_dim(piece, ahead * width, width, 0)
                pieces.append(swap(piece, "seq", far * group + m))
    own = convolve(meta, table, parts, group, True)
    near = {0: own[0]}
    for m in range(1, group):
        near[m] = swap(own[m], "seq", m)
    return finish(meta, [near[m] for m in range(group)] + pieces, group)


def solution(mesh):
    in_specs = (P("seq", "chan"), P(None, None, "chan"), P(None, "seq"))
    out_specs = P("seq", "chan")
    return jax.shard_map(local, mesh=mesh, in_specs=in_specs, out_specs=out_specs, check_vma=False)
```

```python
import functools

import jax
import jax.numpy as jnp
from jax import lax
from jax.experimental import pallas as pl
from jax.experimental.pallas import tpu as pltpu
from jax.sharding import PartitionSpec as P


f32 = jnp.float32
bf16 = jnp.bfloat16
LANES = 128


def swap(value, axis, mask):
    return lax.ppermute(value, axis, [(i, i ^ mask) for i in range(lax.axis_size(axis))])


def advance(value, axis, mask, group):
    pairs = [(i, i ^ mask) for i in range(lax.axis_size(axis))]
    return lax.ppermute(value, axis, [(i, j) for i, j in pairs if i // group < j // group])


def params(mib, axes=1):
    return pltpu.CompilerParams(
        dimension_semantics=("arbitrary",) * axes if axes else None,
        vmem_limit_bytes=mib * 1024 * 1024,
    )


def columns_of(w, place, group, targets):
    sub = w.shape[1] // group
    return jnp.concatenate(
        [w[:, pl.ds(pl.multiple_of((place ^ m) * sub, sub), sub)] for m in targets], axis=1
    )


def project_first_body(meta, mine_ref, w_ref, *refs, group, targets):
    sum_refs, (ahead_ref, mine, held, sems, sem) = refs[:-5], refs[-5:]
    depth = mine_ref.shape[1]
    count = w_ref.shape[0]
    own = pltpu.make_async_copy(mine_ref, mine, sem)
    own.start()

    def fetch(m, k):
        rows = pl.ds(pl.multiple_of((meta[0] ^ m) * depth, depth), depth)
        target = ahead_ref.at[m - 1, k] if m else held.at[k]
        return pltpu.make_async_copy(w_ref.at[k, rows, :], target, sems.at[m, k])

    copies = [[fetch(m, k) for k in range(count)] for m in range(sems.shape[0])]
    for copy in copies[0] + copies[1]:
        copy.start()
    own.wait()
    for k in range(count):
        copies[0][k].wait()
        for later in copies[2:]:
            later[k].start()
        for sum_ref, places in zip(sum_refs, targets, strict=True):
            sum_ref[k] = jnp.dot(
                mine[...],
                columns_of(held.at[k], meta[1], group, places),
                preferred_element_type=f32,
            )
    for copy in [copy for later in copies[1:] for copy in later]:
        copy.wait()


def project_first(meta, mine, weights, chan, group, targets):
    tokens, depth = mine.shape
    count, _, width = weights.shape
    sub = width // group
    vmem, hbm = pl.BlockSpec(memory_space=pltpu.VMEM), pl.BlockSpec(memory_space=pltpu.HBM)
    return pl.pallas_call(
        functools.partial(project_first_body, group=group, targets=targets),
        in_specs=[pl.BlockSpec(memory_space=pltpu.SMEM), hbm, hbm],
        out_specs=[vmem] * (len(targets) + 1),
        scratch_shapes=[
            pltpu.VMEM((tokens, depth), bf16),
            pltpu.VMEM((count, depth, width), bf16),
            pltpu.SemaphoreType.DMA((chan, count)),
            pltpu.SemaphoreType.DMA,
        ],
        out_shape=[
            jax.ShapeDtypeStruct((count, tokens, len(places) * sub), f32) for places in targets
        ]
        + [jax.ShapeDtypeStruct((chan - 1, count, depth, width), bf16)],
        compiler_params=params(32, 0),
        cost_estimate=pl.CostEstimate(
            flops=2 * tokens * depth * width * count,
            bytes_accessed=2 * weights.size,
            transcendentals=0,
        ),
        name="project_first",
    )(meta, pltpu.with_memory_space_constraint(mine, pltpu.HBM), weights)


def project_body(meta, *refs, blocks, group, places, last, riders):
    x_refs, (w_ref, before_ref) = refs[: len(blocks)], refs[len(blocks) : len(blocks) + 2]
    out_refs = refs[len(blocks) + 2 :]
    count, tokens, _ = before_ref.shape
    sub = w_ref.shape[3] // group
    if riders:
        pieces_ref, out_refs = out_refs[0], out_refs[1:]
        pieces = jnp.concatenate([pieces_ref[i] for i in range(pieces_ref.shape[0])])
        out_refs[0][tokens:, :] = jnp.zeros((pieces.shape[0], out_refs[0].shape[1]), bf16)
        out_refs[0][tokens:, 0 : pieces.shape[1]] = pieces.astype(bf16)
    x = jnp.concatenate([x_ref[...] for x_ref in x_refs], axis=1)
    for k in range(count):
        rows = [columns_of(w_ref.at[m - 1, k], meta[1], group, places) for m in blocks]
        total = before_ref[k] + jnp.dot(
            x, jnp.concatenate(rows, axis=0), preferred_element_type=f32
        )
        if last:
            for i, out_ref in enumerate(out_refs):
                out_ref[0:tokens, k * sub : (k + 1) * sub] = total[
                    :, i * sub : (i + 1) * sub
                ].astype(bf16)
        else:
            out_refs[0][k] = total


def project(meta, held, blocks, ahead, before, group, places, last, riders):
    count, tokens, columns = before.shape
    depth = ahead.shape[2]
    width = count * columns // len(places)
    vmem = pl.BlockSpec(memory_space=pltpu.VMEM)
    extra = 0 if riders is None else riders.shape[0] * riders.shape[1]
    if last:
        out_shape = [
            jax.ShapeDtypeStruct((tokens + (0 if i else extra), width), bf16)
            for i in range(len(places))
        ]
    else:
        out_shape = [jax.ShapeDtypeStruct(before.shape, f32)]
    args = [held[m] for m in blocks] + [ahead, before] + ([] if riders is None else [riders])
    return pl.pallas_call(
        functools.partial(
            project_body,
            blocks=blocks,
            group=group,
            places=places,
            last=last,
            riders=riders is not None,
        ),
        in_specs=[pl.BlockSpec(memory_space=pltpu.SMEM)] + [vmem] * len(args),
        out_specs=[vmem] * len(out_shape),
        out_shape=out_shape,
        compiler_params=params(32, 0),
        cost_estimate=pl.CostEstimate(
            flops=2 * tokens * depth * len(blocks) * columns * count,
            bytes_accessed=2 * depth * len(blocks) * columns * count,
            transcendentals=0,
        ),
    )(meta, *args)


def toeplitz_body(meta, pieces_ref, other_ref, out_ref, row, *, order, group):
    count, width = pieces_ref.shape[1:]
    tokens = other_ref.shape[0] - pieces_ref.shape[0] * count
    length = len(order) * width
    step = pl.program_id(0)

    @pl.when(step == 0)
    def _():
        row[:, pl.ds(length, width)] = jnp.zeros((row.shape[0], width), f32)
        across = lax.broadcasted_iota(jnp.int32, (width, width), 0)
        along = lax.broadcasted_iota(jnp.int32, (width, width), 1)
        mirror = (across + along == width - 1).astype(bf16)
        pieces = jnp.concatenate([pieces_ref[i] for i in range(pieces_ref.shape[0])])
        pieces = jnp.concatenate([pieces.astype(bf16), other_ref[tokens:, 0:width]])
        turned = jnp.dot(pieces, mirror, preferred_element_type=f32)
        for at, m in enumerate(order):
            start = length - width * ((meta[3] ^ m) + 1)
            row[0:count, pl.ds(pl.multiple_of(start, width), width)] = turned[
                at * count : (at + 1) * count
            ]

    span = group * width

    @pl.when(step == 0)
    def _():
        out_ref[...] = jnp.zeros(out_ref.shape, bf16)

    @pl.when(step > 0)
    def _():
        start = pl.multiple_of(length - span * step, width)
        for k in range(count):
            line = jnp.broadcast_to(
                row[k : k + 1, pl.ds(start, span + width)], (LANES, span + width)
            )
            turned = pltpu.roll(line, 1, 1, stride=1, stride_axis=0).astype(bf16)
            for e in range(group):
                for h in range(width // LANES):
                    at = span - width * e - LANES * h
                    out_ref[
                        e * width + h * LANES : e * width + (h + 1) * LANES,
                        k * width : (k + 1) * width,
                    ] = turned[:, at : at + width]


def toeplitz(meta, pieces, other, order, group):
    _, count, width = pieces.shape
    blocks = len(order)
    rows, columns = group * width, count * width
    return pl.pallas_call(
        functools.partial(toeplitz_body, order=order, group=group),
        grid_spec=pltpu.PrefetchScalarGridSpec(
            num_scalar_prefetch=1,
            grid=(blocks // group + 1,),
            in_specs=[pl.BlockSpec(memory_space=pltpu.VMEM)] * 2,
            out_specs=pl.BlockSpec((rows, columns), lambda i, meta: (i, 0)),
            scratch_shapes=[pltpu.VMEM((8, (blocks + 1) * width), f32)],
        ),
        out_shape=jax.ShapeDtypeStruct(((blocks + group) * width, columns), bf16),
        compiler_params=params(16),
        cost_estimate=pl.CostEstimate(
            flops=blocks * width * columns * 8,
            bytes_accessed=2 * blocks * width * columns,
            transcendentals=0,
        ),
        name="toeplitz",
    )(meta, pieces, other)


def place_parts(held, p_refs, places, sub, width):
    for p_ref, place in zip(p_refs, places, strict=True):
        at = pl.multiple_of(place * sub, sub)
        for k in range(p_ref.shape[1] // sub):
            held[k * width : (k + 1) * width, pl.ds(at, sub)] = p_ref[0:width, k * sub : (k + 1) * sub]


def pair_sums(rows, group, width, sub):
    return [
        rows[(r + 1) * width : (r + 2) * width, :sub] + rows[r * width : (r + 1) * width, sub:]
        for r in range(group)
    ]


def store_parts(out_refs, placed, sums, place):
    for r, value in enumerate(sums):
        placed[place ^ r] = value.astype(bf16)
    for m, out_ref in enumerate(out_refs):
        out_ref[...] = placed[m]


def convolve_pair_body(meta, table_ref, *refs, at, ahead, group, sub, last):
    p_refs, refs = refs[:2], refs[2:]
    width = p_refs[0].shape[0]
    if last:
        sum_refs, out_refs, (held, placed) = refs[:1], refs[1:-2], refs[-2:]
    else:
        sum_refs, out_refs, (held,) = (), refs[:-1], refs[-1:]
    place = meta[1]
    place_parts(held, p_refs, [place & 1, 1 - (place & 1)], sub, width)
    for i, far in enumerate(ahead):
        start = (far + 1) * group - 1 - 2 * ((place // 2) ^ at)
        rows = table_ref[pl.ds(pl.multiple_of(start * width, width), (group + 1) * width), :]
        sums = pair_sums(
            jnp.dot(rows, held[...], preferred_element_type=f32), group, width, sub
        )
        if last:
            sums = [value + sum_refs[0][r] for r, value in enumerate(sums)]
            store_parts(out_refs, placed, sums, place)
        else:
            for r, value in enumerate(sums):
                out_refs[i][r] = value


def convolve_pair(meta, table, parts, before, at, ahead, group):
    width = parts[0].shape[0]
    columns = table.shape[1]
    sub = parts[0].shape[1] * width // columns
    last = before is not None
    vmem = pl.BlockSpec(memory_space=pltpu.VMEM)
    if last:
        out_shape = [jax.ShapeDtypeStruct((width, sub), bf16)] * group
        scratch = [pltpu.VMEM((group, width, sub), bf16)]
    else:
        out_shape = [jax.ShapeDtypeStruct((group, width, sub), f32)] * len(ahead)
        scratch = []
    args = [table, *parts] + ([before] if last else [])
    return pl.pallas_call(
        functools.partial(
            convolve_pair_body, at=at, ahead=ahead, group=group, sub=sub, last=last
        ),
        in_specs=[pl.BlockSpec(memory_space=pltpu.SMEM)] + [vmem] * len(args),
        out_specs=[vmem] * len(out_shape),
        out_shape=out_shape,
        scratch_shapes=[pltpu.VMEM((columns, 2 * sub), bf16), *scratch],
        compiler_params=params(32, 0),
        cost_estimate=pl.CostEstimate(
            flops=4 * len(ahead) * (group + 1) * width * columns * sub,
            bytes_accessed=2 * width * columns,
            transcendentals=0,
        ),
    )(meta, *args)


def convolve_all_body(meta, low_ref, high_ref, *refs, group, sub):
    p_refs, out_refs, (held, placed) = refs[:group], refs[group : 2 * group], refs[2 * group :]
    width = p_refs[0].shape[0]

    @pl.when(pl.program_id(0) == 0)
    def _():
        place_parts(held, p_refs, [meta[1] ^ m for m in range(group)], sub, width)

    sums = None
    for at in range(0, group, 2):
        side = held[:, at * sub : (at + 2) * sub]
        split = (group - 1 - at) * width
        rows = jnp.concatenate(
            [
                jnp.dot(low_ref[split:, :], side, preferred_element_type=f32),
                jnp.dot(high_ref[: (group - at) * width, :], side, preferred_element_type=f32),
            ]
        )
        more = pair_sums(rows, group, width, sub)
        sums = more if sums is None else [a + b for a, b in zip(sums, more, strict=True)]
    store_parts(out_refs, placed, sums, meta[1])


def convolve_all(meta, table, parts, group):
    width = parts[0].shape[0]
    columns = table.shape[1]
    sub = parts[0].shape[1] * width // columns
    rows = group * width
    steps = table.shape[0] // rows - 1
    return pl.pallas_call(
        functools.partial(convolve_all_body, group=group, sub=sub),
        grid_spec=pltpu.PrefetchScalarGridSpec(
            num_scalar_prefetch=1,
            grid=(steps,),
            in_specs=[
                pl.BlockSpec((rows, columns), lambda i, meta: (i, 0)),
                pl.BlockSpec((rows, columns), lambda i, meta: (i + 1, 0)),
            ]
            + [pl.BlockSpec(part.shape, lambda i, meta: (0, 0)) for part in parts],
            out_specs=[pl.BlockSpec((width, sub), lambda i, meta: (i, 0))] * group,
            scratch_shapes=[
                pltpu.VMEM((columns, group * sub), bf16),
                pltpu.VMEM((group, width, sub), bf16),
            ],
        ),
        out_shape=[jax.ShapeDtypeStruct((steps * width, sub), bf16)] * group,
        compiler_params=params(32),
        cost_estimate=pl.CostEstimate(
            flops=2 * steps * rows * columns * group * sub,
            bytes_accessed=2 * steps * rows * columns,
            transcendentals=0,
        ),
        name="convolve_all",
    )(meta, table, table, *parts)


def finish_body(meta, *refs, group):
    parts, out_ref = refs[:-1], refs[-1]
    sub = out_ref.shape[1] // group
    place = meta[1]
    for m in range(group):
        value = parts[m][...].astype(f32)
        for far in range(1, len(parts) // group):
            value = value + parts[far * group + m][...].astype(f32)
        at = pl.multiple_of((place ^ m) * sub, sub)
        out_ref[:, pl.ds(at, sub)] = value.astype(bf16)


def finish(meta, parts, group):
    width, sub = parts[0].shape
    shape = (width, sub * group)
    return pl.pallas_call(
        functools.partial(finish_body, group=group),
        in_specs=[pl.BlockSpec(memory_space=pltpu.SMEM)]
        + [pl.BlockSpec(memory_space=pltpu.VMEM)] * len(parts),
        out_specs=pl.BlockSpec(memory_space=pltpu.VMEM),
        out_shape=jax.ShapeDtypeStruct(shape, bf16),
        compiler_params=params(24, 0),
        name="finish",
    )(meta, *parts)


def local(inputs, weights, filters):
    seq, chan = lax.axis_size("seq"), lax.axis_size("chan")
    group = min(4, seq)
    groups = seq // group
    width = inputs.shape[0]
    at_seq, at_chan = lax.axis_index("seq"), lax.axis_index("chan")
    lane = jnp.arange(4)
    meta = jnp.where(
        lane == 0,
        at_chan,
        jnp.where(lane == 1, at_seq % group, jnp.where(lane == 2, at_seq // group, at_seq)),
    ).astype(jnp.int32)

    held = {0: inputs}
    held[2] = swap(inputs, "chan", 2)
    held[1] = swap(inputs, "chan", 1)
    held[3] = swap(held[2], "chan", 1)

    weights = pltpu.with_memory_space_constraint(weights, pltpu.HBM)
    pieces = filters[None]
    order = [0]
    bit = seq // 2
    while bit > 1:
        pieces = jnp.concatenate([pieces, swap(pieces, "seq", bit)])
        order += [m ^ bit for m in order]
        bit //= 2
    order += [m ^ 1 for m in order]

    soon = [m for m in range(1, group) if m < 3]
    late = [m for m in range(group) if m not in soon]
    to_soon, to_late, ahead = project_first(meta, inputs, weights, chan, group, [soon, late])
    (to_soon,) = project(meta, held, [1, 2], ahead, to_soon, group, soon, False, None)
    mine = project(meta, held, [3], ahead, to_soon, group, soon, True, pieces)
    mine += project(meta, held, [1, 2, 3], ahead, to_late, group, late, True, None)
    mine = dict(zip(soon + late, mine, strict=True))
    parts = {0: mine[0]}
    for m in range(1, group):
        parts[m] = swap(mine[m], "seq", m)
    parts = [parts[m] for m in range(group)]
    table = toeplitz(meta, pieces, parts[1], order, group)

    if groups == 2 and group == 4:
        sides = [[parts[0], parts[1]], [parts[2], parts[3]]]
        own, after = convolve_pair(meta, table, sides[0], None, 0, (0, 1), group)
        after = convolve_pair(meta, table, sides[1], after, 1, (1,), group)
        own = convolve_pair(meta, table, sides[1], own, 1, (0,), group)
        ahead = {1: after}
    else:
        every = convolve_all(meta, table, [parts[m] for m in range(group)], group)
        own = [every[m][:width] for m in range(group)]
        here = at_seq // group
        ahead = {
            far: [
                lax.dynamic_slice_in_dim(
                    every[m], jnp.maximum((here ^ far) - here, 0) * width, width, 0
                )
                for m in range(group)
            ]
            for far in range(1, groups)
        }
    pieces = [own[0]]
    for m in range(1, group):
        pieces.append(swap(own[m], "seq", m))
    for far in range(1, groups):
        for m in range(group):
            pieces.append(advance(ahead[far][m], "seq", far * group + m, group))
    return finish(meta, pieces, group)


def solution(mesh):
    in_specs = (P("seq", "chan"), P(None, None, "chan"), P(None, "seq"))
    out_specs = P("seq", "chan")
    return jax.shard_map(local, mesh=mesh, in_specs=in_specs, out_specs=out_specs, check_vma=False)
```

```python
import functools

import jax
import jax.numpy as jnp
from jax import lax
from jax.experimental import pallas as pl
from jax.experimental.pallas import tpu as pltpu
from jax.sharding import PartitionSpec as P


f32 = jnp.float32
bf16 = jnp.bfloat16
LANES = 128


def swap(value, axis, mask):
    return lax.ppermute(value, axis, [(i, i ^ mask) for i in range(lax.axis_size(axis))])


def params(mib, axes=1):
    return pltpu.CompilerParams(
        dimension_semantics=("arbitrary",) * axes if axes else None,
        vmem_limit_bytes=mib * 1024 * 1024,
    )


def columns_of(w, place, group, targets):
    sub = w.shape[1] // group
    return jnp.concatenate(
        [w[:, pl.ds(pl.multiple_of((place ^ m) * sub, sub), sub)] for m in targets], axis=1
    )


def project_first_body(meta, mine_ref, w_ref, *refs, group, targets):
    sum_refs, (ahead_ref, mine, held, sems, sem) = refs[:-5], refs[-5:]
    depth = mine_ref.shape[1]
    count = w_ref.shape[0]
    own = pltpu.make_async_copy(mine_ref, mine, sem)
    own.start()

    def fetch(m, k):
        rows = pl.ds(pl.multiple_of((meta[0] ^ m) * depth, depth), depth)
        target = ahead_ref.at[m - 1, k] if m else held.at[k]
        return pltpu.make_async_copy(w_ref.at[k, rows, :], target, sems.at[m, k])

    copies = [[fetch(m, k) for k in range(count)] for m in range(sems.shape[0])]
    for copy in copies[0]:
        copy.start()
    own.wait()
    for k in range(count):
        copies[0][k].wait()
        if k == 0:
            for copy in [copy for later in copies[1:] for copy in later]:
                copy.start()
        for sum_ref, places in zip(sum_refs, targets, strict=True):
            sum_ref[k] = jnp.dot(
                mine[...],
                columns_of(held.at[k], meta[1], group, places),
                preferred_element_type=f32,
            )
    for copy in [copy for later in copies[1:] for copy in later]:
        copy.wait()


def project_first(meta, mine, weights, chan, group, targets):
    tokens, depth = mine.shape
    count, _, width = weights.shape
    sub = width // group
    vmem, hbm = pl.BlockSpec(memory_space=pltpu.VMEM), pl.BlockSpec(memory_space=pltpu.HBM)
    return pl.pallas_call(
        functools.partial(project_first_body, group=group, targets=targets),
        in_specs=[pl.BlockSpec(memory_space=pltpu.SMEM), hbm, hbm],
        out_specs=[vmem] * (len(targets) + 1),
        scratch_shapes=[
            pltpu.VMEM((tokens, depth), bf16),
            pltpu.VMEM((count, depth, width), bf16),
            pltpu.SemaphoreType.DMA((chan, count)),
            pltpu.SemaphoreType.DMA,
        ],
        out_shape=[
            jax.ShapeDtypeStruct((count, tokens, len(places) * sub), f32) for places in targets
        ]
        + [jax.ShapeDtypeStruct((chan - 1, count, depth, width), bf16)],
        compiler_params=params(32, 0),
        cost_estimate=pl.CostEstimate(
            flops=2 * tokens * depth * width * count,
            bytes_accessed=2 * weights.size,
            transcendentals=0,
        ),
        name="project_first",
    )(meta, pltpu.with_memory_space_constraint(mine, pltpu.HBM), weights)


def project_body(meta, *refs, blocks, group, places, last, riders):
    x_refs, (w_ref, before_ref) = refs[: len(blocks)], refs[len(blocks) : len(blocks) + 2]
    out_refs = refs[len(blocks) + 2 :]
    count, tokens, _ = before_ref.shape
    sub = w_ref.shape[3] // group
    if riders:
        pieces_ref, out_refs = out_refs[0], out_refs[1:]
        pieces = jnp.concatenate([pieces_ref[i] for i in range(pieces_ref.shape[0])])
        for out_ref in out_refs:
            out_ref[tokens:, :] = jnp.zeros((pieces.shape[0], out_ref.shape[1]), bf16)
            out_ref[tokens:, 0 : pieces.shape[1]] = pieces.astype(bf16)
    x = jnp.concatenate([x_ref[...] for x_ref in x_refs], axis=1)
    for k in range(count):
        rows = [columns_of(w_ref.at[m - 1, k], meta[1], group, places) for m in blocks]
        total = before_ref[k] + jnp.dot(
            x, jnp.concatenate(rows, axis=0), preferred_element_type=f32
        )
        if last:
            for i, out_ref in enumerate(out_refs):
                out_ref[0:tokens, k * sub : (k + 1) * sub] = total[
                    :, i * sub : (i + 1) * sub
                ].astype(bf16)
        else:
            out_refs[0][k] = total


def project(meta, held, blocks, ahead, before, group, places, last, riders):
    count, tokens, columns = before.shape
    depth = ahead.shape[2]
    width = count * columns // len(places)
    vmem = pl.BlockSpec(memory_space=pltpu.VMEM)
    extra = 0 if riders is None else riders.shape[0] * riders.shape[1]
    if last:
        out_shape = [
            jax.ShapeDtypeStruct((tokens + extra, width), bf16) for _ in places
        ]
    else:
        out_shape = [jax.ShapeDtypeStruct(before.shape, f32)]
    args = [held[m] for m in blocks] + [ahead, before] + ([] if riders is None else [riders])
    return pl.pallas_call(
        functools.partial(
            project_body,
            blocks=blocks,
            group=group,
            places=places,
            last=last,
            riders=riders is not None,
        ),
        in_specs=[pl.BlockSpec(memory_space=pltpu.SMEM)] + [vmem] * len(args),
        out_specs=[vmem] * len(out_shape),
        out_shape=out_shape,
        compiler_params=params(32, 0),
        cost_estimate=pl.CostEstimate(
            flops=2 * tokens * depth * len(blocks) * columns * count,
            bytes_accessed=2 * depth * len(blocks) * columns * count,
            transcendentals=0,
        ),
    )(meta, *args)


def toeplitz_body(meta, *refs, order, group):
    (pieces_ref, far_ref), rider_refs, (out_ref, row) = refs[:2], refs[2:-2], refs[-2:]
    count, width = pieces_ref.shape[1:]
    slices = pieces_ref.shape[0]
    tokens = rider_refs[0].shape[0] - slices * count
    length = len(order) * width
    step = pl.program_id(0)

    @pl.when(step == 0)
    def _():
        row[:, pl.ds(length, width)] = jnp.zeros((row.shape[0], width), f32)
        across = lax.broadcasted_iota(jnp.int32, (width, width), 0)
        along = lax.broadcasted_iota(jnp.int32, (width, width), 1)
        mirror = (across + along == width - 1).astype(bf16)
        near, far = [
            jnp.concatenate([ref[i] for i in range(slices)]).astype(bf16)
            for ref in (pieces_ref, far_ref)
        ]
        riders = [ref[tokens:, 0:width] for ref in rider_refs]
        pieces = jnp.concatenate([near, *riders, far])
        turned = jnp.dot(pieces, mirror, preferred_element_type=f32)
        for at, m in enumerate(order):
            start = length - width * ((meta[3] ^ m) + 1)
            row[0:count, pl.ds(pl.multiple_of(start, width), width)] = turned[
                at * count : (at + 1) * count
            ]

    span = group * width

    @pl.when(step == 0)
    def _():
        out_ref[...] = jnp.zeros(out_ref.shape, bf16)

    @pl.when(step > 0)
    def _():
        start = pl.multiple_of(length - span * step, width)
        for k in range(count):
            line = jnp.broadcast_to(
                row[k : k + 1, pl.ds(start, span + width)], (LANES, span + width)
            )
            turned = pltpu.roll(line, 1, 1, stride=1, stride_axis=0).astype(bf16)
            for e in range(group):
                for h in range(width // LANES):
                    at = span - width * e - LANES * h
                    out_ref[
                        e * width + h * LANES : e * width + (h + 1) * LANES,
                        k * width : (k + 1) * width,
                    ] = turned[:, at : at + width]


def toeplitz(meta, pieces, far, riders, order, group):
    _, count, width = pieces.shape
    blocks = len(order)
    rows, columns = group * width, count * width
    return pl.pallas_call(
        functools.partial(toeplitz_body, order=order, group=group),
        grid_spec=pltpu.PrefetchScalarGridSpec(
            num_scalar_prefetch=1,
            grid=(blocks // group + 1,),
            in_specs=[pl.BlockSpec(memory_space=pltpu.VMEM)] * (2 + len(riders)),
            out_specs=pl.BlockSpec((rows, columns), lambda i, meta: (i, 0)),
            scratch_shapes=[pltpu.VMEM((8, (blocks + 1) * width), f32)],
        ),
        out_shape=jax.ShapeDtypeStruct(((blocks + group) * width, columns), bf16),
        compiler_params=params(16),
        cost_estimate=pl.CostEstimate(
            flops=blocks * width * columns * 8,
            bytes_accessed=2 * blocks * width * columns,
            transcendentals=0,
        ),
        name="toeplitz",
    )(meta, pieces, far, *riders)


def place_parts(held, p_refs, places, sub, width):
    for p_ref, place in zip(p_refs, places, strict=True):
        at = pl.multiple_of(place * sub, sub)
        for k in range(p_ref.shape[1] // sub):
            held[k * width : (k + 1) * width, pl.ds(at, sub)] = p_ref[0:width, k * sub : (k + 1) * sub]


def pair_sums(rows, group, width, sub):
    return [
        rows[(r + 1) * width : (r + 2) * width, :sub] + rows[r * width : (r + 1) * width, sub:]
        for r in range(group)
    ]


def store_parts(out_refs, placed, sums, place):
    for r, value in enumerate(sums):
        placed[place ^ r] = value.astype(bf16)
    for m, out_ref in enumerate(out_refs):
        out_ref[...] = placed[m]


def convolve_pair_body(meta, table_ref, *refs, at, ahead, group, sub, last):
    p_refs, refs = refs[:2], refs[2:]
    width = min(p_ref.shape[0] for p_ref in p_refs)
    if last:
        sum_refs, out_refs, (held, placed) = refs[:1], refs[1:-2], refs[-2:]
    else:
        sum_refs, out_refs, (held,) = (), refs[:-1], refs[-1:]
    place = meta[1]
    place_parts(held, p_refs, [place & 1, 1 - (place & 1)], sub, width)
    for i, far in enumerate(ahead):
        start = (far + 1) * group - 1 - 2 * ((place // 2) ^ at)
        rows = table_ref[pl.ds(pl.multiple_of(start * width, width), (group + 1) * width), :]
        sums = pair_sums(
            jnp.dot(rows, held[...], preferred_element_type=f32), group, width, sub
        )
        if last:
            sums = [value + sum_refs[0][r] for r, value in enumerate(sums)]
            store_parts(out_refs, placed, sums, place)
        else:
            for r, value in enumerate(sums):
                out_refs[i][r] = value


def convolve_pair(meta, table, parts, before, at, ahead, group):
    width = min(part.shape[0] for part in parts)
    columns = table.shape[1]
    sub = parts[0].shape[1] * width // columns
    last = before is not None
    vmem = pl.BlockSpec(memory_space=pltpu.VMEM)
    if last:
        out_shape = [jax.ShapeDtypeStruct((width, sub), bf16)] * group
        scratch = [pltpu.VMEM((group, width, sub), bf16)]
    else:
        out_shape = [jax.ShapeDtypeStruct((group, width, sub), f32)] * len(ahead)
        scratch = []
    args = [table, *parts] + ([before] if last else [])
    return pl.pallas_call(
        functools.partial(
            convolve_pair_body, at=at, ahead=ahead, group=group, sub=sub, last=last
        ),
        in_specs=[pl.BlockSpec(memory_space=pltpu.SMEM)] + [vmem] * len(args),
        out_specs=[vmem] * len(out_shape),
        out_shape=out_shape,
        scratch_shapes=[pltpu.VMEM((columns, 2 * sub), bf16), *scratch],
        compiler_params=params(32, 0),
        cost_estimate=pl.CostEstimate(
            flops=4 * len(ahead) * (group + 1) * width * columns * sub,
            bytes_accessed=2 * width * columns,
            transcendentals=0,
        ),
    )(meta, *args)


def convolve_all_body(meta, low_ref, high_ref, *refs, group, sub):
    p_refs, out_refs, (held, placed) = refs[:group], refs[group : 2 * group], refs[2 * group :]
    width = p_refs[0].shape[0]

    @pl.when(pl.program_id(0) == 0)
    def _():
        place_parts(held, p_refs, [meta[1] ^ m for m in range(group)], sub, width)

    sums = None
    for at in range(0, group, 2):
        side = held[:, at * sub : (at + 2) * sub]
        split = (group - 1 - at) * width
        rows = jnp.concatenate(
            [
                jnp.dot(low_ref[split:, :], side, preferred_element_type=f32),
                jnp.dot(high_ref[: (group - at) * width, :], side, preferred_element_type=f32),
            ]
        )
        more = pair_sums(rows, group, width, sub)
        sums = more if sums is None else [a + b for a, b in zip(sums, more, strict=True)]
    store_parts(out_refs, placed, sums, meta[1])


def convolve_all(meta, table, parts, group):
    width = parts[0].shape[0]
    columns = table.shape[1]
    sub = parts[0].shape[1] * width // columns
    rows = group * width
    steps = table.shape[0] // rows - 1
    return pl.pallas_call(
        functools.partial(convolve_all_body, group=group, sub=sub),
        grid_spec=pltpu.PrefetchScalarGridSpec(
            num_scalar_prefetch=1,
            grid=(steps,),
            in_specs=[
                pl.BlockSpec((rows, columns), lambda i, meta: (i, 0)),
                pl.BlockSpec((rows, columns), lambda i, meta: (i + 1, 0)),
            ]
            + [pl.BlockSpec(part.shape, lambda i, meta: (0, 0)) for part in parts],
            out_specs=[pl.BlockSpec((width, sub), lambda i, meta: (i, 0))] * group,
            scratch_shapes=[
                pltpu.VMEM((columns, group * sub), bf16),
                pltpu.VMEM((group, width, sub), bf16),
            ],
        ),
        out_shape=[jax.ShapeDtypeStruct((steps * width, sub), bf16)] * group,
        compiler_params=params(32),
        cost_estimate=pl.CostEstimate(
            flops=2 * steps * rows * columns * group * sub,
            bytes_accessed=2 * steps * rows * columns,
            transcendentals=0,
        ),
        name="convolve_all",
    )(meta, table, table, *parts)


def finish_body(meta, *refs, group):
    parts, out_ref = refs[:-1], refs[-1]
    sub = out_ref.shape[1] // group
    place, own = meta[1], meta[2]
    for m in range(group):
        value = parts[m][...].astype(f32)
        for far in range(1, len(parts) // group):
            other = parts[far * group + m][...].astype(f32)
            value = value + jnp.where((own ^ far) < own, other, 0.0)
        at = pl.multiple_of((place ^ m) * sub, sub)
        out_ref[:, pl.ds(at, sub)] = value.astype(bf16)


def finish(meta, parts, group):
    width, sub = parts[0].shape
    shape = (width, sub * group)
    return pl.pallas_call(
        functools.partial(finish_body, group=group),
        in_specs=[pl.BlockSpec(memory_space=pltpu.SMEM)]
        + [pl.BlockSpec(memory_space=pltpu.VMEM)] * len(parts),
        out_specs=pl.BlockSpec(memory_space=pltpu.VMEM),
        out_shape=jax.ShapeDtypeStruct(shape, bf16),
        compiler_params=params(24, 0),
        name="finish",
    )(meta, *parts)


def local(inputs, weights, filters):
    seq, chan = lax.axis_size("seq"), lax.axis_size("chan")
    group = min(4, seq)
    groups = seq // group
    width = inputs.shape[0]
    at_seq, at_chan = lax.axis_index("seq"), lax.axis_index("chan")
    lane = jnp.arange(4)
    meta = jnp.where(
        lane == 0,
        at_chan,
        jnp.where(lane == 1, at_seq % group, jnp.where(lane == 2, at_seq // group, at_seq)),
    ).astype(jnp.int32)

    held = {0: inputs}
    held[2] = swap(inputs, "chan", 2)
    held[1] = swap(inputs, "chan", 1)
    held[3] = swap(held[2], "chan", 1)

    weights = pltpu.with_memory_space_constraint(weights, pltpu.HBM)
    pieces = filters[None]
    order = [0]
    bit = seq // 2
    while bit >= group:
        pieces = jnp.concatenate([pieces, swap(pieces, "seq", bit)])
        order += [m ^ bit for m in order]
        bit //= 2
    order = [m ^ near for near in range(group) for m in order]

    soon = [m for m in range(1, group) if m < 3]
    late = [m for m in range(group) if m not in soon]
    to_soon, to_late, ahead = project_first(meta, inputs, weights, chan, group, [soon, late])
    (to_soon,) = project(meta, held, [1, 2], ahead, to_soon, group, soon, False, None)
    mine = project(meta, held, [3], ahead, to_soon, group, soon, True, pieces)
    mine += project(meta, held, [1, 2, 3], ahead, to_late, group, late, True, None)
    mine = dict(zip(soon + late, mine, strict=True))
    parts = {0: mine[0]}
    for m in range(1, group):
        parts[m] = swap(mine[m], "seq", m)
    parts = [parts[m] for m in range(group)]
    far_pieces = swap(pieces, "seq", 3)
    table = toeplitz(meta, pieces, far_pieces, parts[1:3], order, group)

    if groups == 2 and group == 4:
        sides = [[parts[0], parts[1]], [parts[2], parts[3]]]
        own, after = convolve_pair(meta, table, sides[0], None, 0, (0, 1), group)
        after = convolve_pair(meta, table, sides[1], after, 1, (1,), group)
        own = convolve_pair(meta, table, sides[1], own, 1, (0,), group)
        ahead = {1: after}
    else:
        every = convolve_all(meta, table, [parts[m] for m in range(group)], group)
        own = [every[m][:width] for m in range(group)]
        here = at_seq // group
        ahead = {
            far: [
                lax.dynamic_slice_in_dim(
                    every[m], jnp.maximum((here ^ far) - here, 0) * width, width, 0
                )
                for m in range(group)
            ]
            for far in range(1, groups)
        }
    pieces = [own[0]]
    for m in range(1, group):
        pieces.append(swap(own[m], "seq", m))
    for far in range(1, groups):
        for m in range(group):
            pieces.append(swap(ahead[far][m], "seq", far * group + m))
    return finish(meta, pieces, group)


def solution(mesh):
    in_specs = (P("seq", "chan"), P(None, None, "chan"), P(None, "seq"))
    out_specs = P("seq", "chan")
    return jax.shard_map(local, mesh=mesh, in_specs=in_specs, out_specs=out_specs, check_vma=False)
```

```python
import jax
import jax.numpy as jnp
from jax import lax
from jax.experimental import pallas as pl
from jax.experimental.pallas import tpu as pltpu
from jax.sharding import PartitionSpec as P


f32 = jnp.float32
bf16 = jnp.bfloat16
LANES = 128


def swap(value, axis, mask):
    return lax.ppermute(value, axis, [(i, i ^ mask) for i in range(lax.axis_size(axis))])


def params(mib, axes=1):
    return pltpu.CompilerParams(
        dimension_semantics=("arbitrary",) * axes if axes else None,
        vmem_limit_bytes=mib * 1024 * 1024,
    )


def on_device(body, group, **settings):
    def kernel(*refs):
        seq = lax.axis_index("seq")
        place, own = seq & (group - 1), lax.shift_right_logical(seq, group.bit_length() - 1)
        body((lax.axis_index("chan"), place, own, seq), *refs, group=group, **settings)

    return kernel


def columns_of(w, place, group, targets):
    sub = w.shape[1] // group
    return jnp.concatenate(
        [w[:, pl.ds(pl.multiple_of((place ^ m) * sub, sub), sub)] for m in targets], axis=1
    )


def project_first_body(meta, mine_ref, w_ref, *refs, group, targets):
    sum_refs, (ahead_ref, mine, held, sems, sem) = refs[:-5], refs[-5:]
    depth = mine_ref.shape[1]
    count = w_ref.shape[0]
    own = pltpu.make_async_copy(mine_ref, mine, sem)
    own.start()

    def fetch(m, k):
        rows = pl.ds(pl.multiple_of((meta[0] ^ m) * depth, depth), depth)
        target = ahead_ref.at[m - 1, k] if m else held.at[k]
        return pltpu.make_async_copy(w_ref.at[k, rows, :], target, sems.at[m, k])

    copies = [[fetch(m, k) for k in range(count)] for m in range(sems.shape[0])]
    for copy in copies[0]:
        copy.start()
    own.wait()
    for k in range(count):
        copies[0][k].wait()
        if k == 0:
            for copy in [copy for later in copies[1:] for copy in later]:
                copy.start()
        for sum_ref, places in zip(sum_refs, targets, strict=True):
            sum_ref[k] = jnp.dot(
                mine[...],
                columns_of(held.at[k], meta[1], group, places),
                preferred_element_type=f32,
            )
    for copy in [copy for later in copies[1:] for copy in later]:
        copy.wait()


def project_first(mine, weights, chan, group, targets):
    tokens, depth = mine.shape
    count, _, width = weights.shape
    sub = width // group
    vmem, hbm = pl.BlockSpec(memory_space=pltpu.VMEM), pl.BlockSpec(memory_space=pltpu.HBM)
    return pl.pallas_call(
        on_device(project_first_body, group=group, targets=targets),
        in_specs=[hbm, hbm],
        out_specs=[vmem] * (len(targets) + 1),
        scratch_shapes=[
            pltpu.VMEM((tokens, depth), bf16),
            pltpu.VMEM((count, depth, width), bf16),
            pltpu.SemaphoreType.DMA((chan, count)),
            pltpu.SemaphoreType.DMA,
        ],
        out_shape=[
            jax.ShapeDtypeStruct((count, tokens, len(places) * sub), f32) for places in targets
        ]
        + [jax.ShapeDtypeStruct((chan - 1, count, depth, width), bf16)],
        compiler_params=params(32, 0),
        cost_estimate=pl.CostEstimate(
            flops=2 * tokens * depth * width * count,
            bytes_accessed=2 * weights.size,
            transcendentals=0,
        ),
        name="project_first",
    )(pltpu.with_memory_space_constraint(mine, pltpu.HBM), weights)


def project_body(meta, *refs, blocks, group, places, last, riders):
    x_refs, (w_ref, before_ref) = refs[: len(blocks)], refs[len(blocks) : len(blocks) + 2]
    out_refs = refs[len(blocks) + 2 :]
    count, tokens, _ = before_ref.shape
    sub = w_ref.shape[3] // group
    if riders:
        pieces_ref, out_refs = out_refs[0], out_refs[1:]
        pieces = jnp.concatenate([pieces_ref[i] for i in range(pieces_ref.shape[0])])
        for out_ref in out_refs:
            out_ref[tokens:, :] = jnp.zeros((pieces.shape[0], out_ref.shape[1]), bf16)
            out_ref[tokens:, 0 : pieces.shape[1]] = pieces.astype(bf16)
    x = jnp.concatenate([x_ref[...] for x_ref in x_refs], axis=1)
    for k in range(count):
        rows = [columns_of(w_ref.at[m - 1, k], meta[1], group, places) for m in blocks]
        total = before_ref[k] + jnp.dot(
            x, jnp.concatenate(rows, axis=0), preferred_element_type=f32
        )
        if last:
            for i, out_ref in enumerate(out_refs):
                out_ref[0:tokens, k * sub : (k + 1) * sub] = total[
                    :, i * sub : (i + 1) * sub
                ].astype(bf16)
        else:
            out_refs[0][k] = total


def project(held, blocks, ahead, before, group, places, last, riders):
    count, tokens, columns = before.shape
    depth = ahead.shape[2]
    width = count * columns // len(places)
    vmem = pl.BlockSpec(memory_space=pltpu.VMEM)
    extra = 0 if riders is None else riders.shape[0] * riders.shape[1]
    if last:
        out_shape = [
            jax.ShapeDtypeStruct((tokens + extra, width), bf16) for _ in places
        ]
    else:
        out_shape = [jax.ShapeDtypeStruct(before.shape, f32)]
    args = [held[m] for m in blocks] + [ahead, before] + ([] if riders is None else [riders])
    return pl.pallas_call(
        on_device(project_body, blocks=blocks,
            group=group,
            places=places,
            last=last,
            riders=riders is not None,
        ),
        in_specs=[vmem] * len(args),
        out_specs=[vmem] * len(out_shape),
        out_shape=out_shape,
        compiler_params=params(32, 0),
        cost_estimate=pl.CostEstimate(
            flops=2 * tokens * depth * len(blocks) * columns * count,
            bytes_accessed=2 * depth * len(blocks) * columns * count,
            transcendentals=0,
        ),
    )(*args)


def toeplitz_body(meta, *refs, order, group):
    (pieces_ref, far_ref), rider_refs, (out_ref, row) = refs[:2], refs[2:-2], refs[-2:]
    count, width = pieces_ref.shape[1:]
    slices = pieces_ref.shape[0]
    tokens = rider_refs[0].shape[0] - slices * count
    length = len(order) * width
    step = pl.program_id(0)

    @pl.when(step == 0)
    def _():
        row[:, pl.ds(length, width)] = jnp.zeros((row.shape[0], width), f32)
        across = lax.broadcasted_iota(jnp.int32, (width, width), 0)
        along = lax.broadcasted_iota(jnp.int32, (width, width), 1)
        mirror = (across + along == width - 1).astype(bf16)
        near, far = [
            jnp.concatenate([ref[i] for i in range(slices)]).astype(bf16)
            for ref in (pieces_ref, far_ref)
        ]
        riders = [ref[tokens:, 0:width] for ref in rider_refs]
        pieces = jnp.concatenate([near, *riders, far])
        turned = jnp.dot(pieces, mirror, preferred_element_type=f32)
        for at, m in enumerate(order):
            start = length - width * ((meta[3] ^ m) + 1)
            row[0:count, pl.ds(pl.multiple_of(start, width), width)] = turned[
                at * count : (at + 1) * count
            ]

    span = group * width

    @pl.when(step == 0)
    def _():
        out_ref[...] = jnp.zeros(out_ref.shape, bf16)

    @pl.when(step > 0)
    def _():
        start = pl.multiple_of(length - span * step, width)
        for k in range(count):
            line = jnp.broadcast_to(
                row[k : k + 1, pl.ds(start, span + width)], (LANES, span + width)
            )
            turned = pltpu.roll(line, 1, 1, stride=1, stride_axis=0).astype(bf16)
            for e in range(group):
                for h in range(width // LANES):
                    at = span - width * e - LANES * h
                    out_ref[
                        e * width + h * LANES : e * width + (h + 1) * LANES,
                        k * width : (k + 1) * width,
                    ] = turned[:, at : at + width]


def toeplitz(pieces, far, riders, order, group):
    _, count, width = pieces.shape
    blocks = len(order)
    rows, columns = group * width, count * width
    return pl.pallas_call(
        on_device(toeplitz_body, order=order, group=group),
        grid_spec=pltpu.PrefetchScalarGridSpec(
            num_scalar_prefetch=0,
            grid=(blocks // group + 1,),
            in_specs=[pl.BlockSpec(memory_space=pltpu.VMEM)] * (2 + len(riders)),
            out_specs=pl.BlockSpec((rows, columns), lambda i: (i, 0)),
            scratch_shapes=[pltpu.VMEM((8, (blocks + 1) * width), f32)],
        ),
        out_shape=jax.ShapeDtypeStruct(((blocks + group) * width, columns), bf16),
        compiler_params=params(16),
        cost_estimate=pl.CostEstimate(
            flops=blocks * width * columns * 8,
            bytes_accessed=2 * blocks * width * columns,
            transcendentals=0,
        ),
        name="toeplitz",
    )(pieces, far, *riders)


def place_parts(held, p_refs, places, sub, width):
    for p_ref, place in zip(p_refs, places, strict=True):
        at = pl.multiple_of(place * sub, sub)
        for k in range(p_ref.shape[1] // sub):
            held[k * width : (k + 1) * width, pl.ds(at, sub)] = p_ref[0:width, k * sub : (k + 1) * sub]


def pair_sums(rows, group, width, sub):
    return [
        rows[(r + 1) * width : (r + 2) * width, :sub] + rows[r * width : (r + 1) * width, sub:]
        for r in range(group)
    ]


def store_parts(out_refs, placed, sums, place):
    for r, value in enumerate(sums):
        placed[place ^ r] = value.astype(bf16)
    for m, out_ref in enumerate(out_refs):
        out_ref[...] = placed[m]


def convolve_pair_body(meta, table_ref, *refs, at, ahead, group, sub, last):
    p_refs, refs = refs[:2], refs[2:]
    width = min(p_ref.shape[0] for p_ref in p_refs)
    if last:
        sum_refs, out_refs, (held, placed) = refs[:1], refs[1:-2], refs[-2:]
    else:
        sum_refs, out_refs, (held,) = (), refs[:-1], refs[-1:]
    place = meta[1]
    place_parts(held, p_refs, [place & 1, 1 - (place & 1)], sub, width)
    for i, far in enumerate(ahead):
        start = (far + 1) * group - 1 - 2 * ((place // 2) ^ at)
        rows = table_ref[pl.ds(pl.multiple_of(start * width, width), (group + 1) * width), :]
        sums = pair_sums(
            jnp.dot(rows, held[...], preferred_element_type=f32), group, width, sub
        )
        if last:
            sums = [value + sum_refs[0][r] for r, value in enumerate(sums)]
            store_parts(out_refs, placed, sums, place)
        else:
            for r, value in enumerate(sums):
                out_refs[i][r] = value


def convolve_pair(table, parts, before, at, ahead, group):
    width = min(part.shape[0] for part in parts)
    columns = table.shape[1]
    sub = parts[0].shape[1] * width // columns
    last = before is not None
    vmem = pl.BlockSpec(memory_space=pltpu.VMEM)
    if last:
        out_shape = [jax.ShapeDtypeStruct((width, sub), bf16)] * group
        scratch = [pltpu.VMEM((group, width, sub), bf16)]
    else:
        out_shape = [jax.ShapeDtypeStruct((group, width, sub), f32)] * len(ahead)
        scratch = []
    args = [table, *parts] + ([before] if last else [])
    return pl.pallas_call(
        on_device(convolve_pair_body, at=at, ahead=ahead, group=group, sub=sub, last=last
        ),
        in_specs=[vmem] * len(args),
        out_specs=[vmem] * len(out_shape),
        out_shape=out_shape,
        scratch_shapes=[pltpu.VMEM((columns, 2 * sub), bf16), *scratch],
        compiler_params=params(32, 0),
        cost_estimate=pl.CostEstimate(
            flops=4 * len(ahead) * (group + 1) * width * columns * sub,
            bytes_accessed=2 * width * columns,
            transcendentals=0,
        ),
    )(*args)


def convolve_all_body(meta, low_ref, high_ref, *refs, group, sub):
    p_refs, out_refs, (held, placed) = refs[:group], refs[group : 2 * group], refs[2 * group :]
    width = p_refs[0].shape[0]

    @pl.when(pl.program_id(0) == 0)
    def _():
        place_parts(held, p_refs, [meta[1] ^ m for m in range(group)], sub, width)

    sums = None
    for at in range(0, group, 2):
        side = held[:, at * sub : (at + 2) * sub]
        split = (group - 1 - at) * width
        rows = jnp.concatenate(
            [
                jnp.dot(low_ref[split:, :], side, preferred_element_type=f32),
                jnp.dot(high_ref[: (group - at) * width, :], side, preferred_element_type=f32),
            ]
        )
        more = pair_sums(rows, group, width, sub)
        sums = more if sums is None else [a + b for a, b in zip(sums, more, strict=True)]
    store_parts(out_refs, placed, sums, meta[1])


def convolve_all(table, parts, group):
    width = parts[0].shape[0]
    columns = table.shape[1]
    sub = parts[0].shape[1] * width // columns
    rows = group * width
    steps = table.shape[0] // rows - 1
    return pl.pallas_call(
        on_device(convolve_all_body, group=group, sub=sub),
        grid_spec=pltpu.PrefetchScalarGridSpec(
            num_scalar_prefetch=0,
            grid=(steps,),
            in_specs=[
                pl.BlockSpec((rows, columns), lambda i: (i, 0)),
                pl.BlockSpec((rows, columns), lambda i: (i + 1, 0)),
            ]
            + [pl.BlockSpec(part.shape, lambda i: (0, 0)) for part in parts],
            out_specs=[pl.BlockSpec((width, sub), lambda i: (i, 0))] * group,
            scratch_shapes=[
                pltpu.VMEM((columns, group * sub), bf16),
                pltpu.VMEM((group, width, sub), bf16),
            ],
        ),
        out_shape=[jax.ShapeDtypeStruct((steps * width, sub), bf16)] * group,
        compiler_params=params(32),
        cost_estimate=pl.CostEstimate(
            flops=2 * steps * rows * columns * group * sub,
            bytes_accessed=2 * steps * rows * columns,
            transcendentals=0,
        ),
        name="convolve_all",
    )(table, table, *parts)


def finish_body(meta, *refs, group):
    parts, out_ref = refs[:-1], refs[-1]
    sub = out_ref.shape[1] // group
    place, own = meta[1], meta[2]
    for m in range(group):
        value = parts[m][...].astype(f32)
        for far in range(1, len(parts) // group):
            other = parts[far * group + m][...].astype(f32)
            value = value + jnp.where((own ^ far) < own, other, 0.0)
        at = pl.multiple_of((place ^ m) * sub, sub)
        out_ref[:, pl.ds(at, sub)] = value.astype(bf16)


def finish(parts, group):
    width, sub = parts[0].shape
    shape = (width, sub * group)
    return pl.pallas_call(
        on_device(finish_body, group=group),
        in_specs=[pl.BlockSpec(memory_space=pltpu.VMEM)] * len(parts),
        out_specs=pl.BlockSpec(memory_space=pltpu.VMEM),
        out_shape=jax.ShapeDtypeStruct(shape, bf16),
        compiler_params=params(24, 0),
        name="finish",
    )(*parts)


def local(inputs, weights, filters):
    seq, chan = lax.axis_size("seq"), lax.axis_size("chan")
    group = min(4, seq)
    groups = seq // group
    width = inputs.shape[0]
    at_seq = lax.axis_index("seq")
    held = {0: inputs}
    held[2] = swap(inputs, "chan", 2)
    held[1] = swap(inputs, "chan", 1)
    held[3] = swap(held[2], "chan", 1)

    weights = pltpu.with_memory_space_constraint(weights, pltpu.HBM)
    pieces = filters[None]
    order = [0]
    bit = seq // 2
    while bit >= group:
        pieces = jnp.concatenate([pieces, swap(pieces, "seq", bit)])
        order += [m ^ bit for m in order]
        bit //= 2
    order = [m ^ near for near in range(group) for m in order]

    soon = [m for m in range(1, group) if m < 3]
    late = [m for m in range(group) if m not in soon]
    to_soon, to_late, ahead = project_first(inputs, weights, chan, group, [soon, late])
    (to_soon,) = project(held, [1, 2], ahead, to_soon, group, soon, False, None)
    mine = project(held, [3], ahead, to_soon, group, soon, True, pieces)
    mine += project(held, [1, 2, 3], ahead, to_late, group, late, True, None)
    mine = dict(zip(soon + late, mine, strict=True))
    parts = {0: mine[0]}
    for m in range(1, group):
        parts[m] = swap(mine[m], "seq", m)
    parts = [parts[m] for m in range(group)]
    far_pieces = swap(pieces, "seq", 3)
    table = toeplitz(pieces, far_pieces, parts[1:3], order, group)

    if groups == 2 and group == 4:
        sides = [[parts[0], parts[1]], [parts[2], parts[3]]]
        own, after = convolve_pair(table, sides[0], None, 0, (0, 1), group)
        after = convolve_pair(table, sides[1], after, 1, (1,), group)
        own = convolve_pair(table, sides[1], own, 1, (0,), group)
        ahead = {1: after}
    else:
        every = convolve_all(table, [parts[m] for m in range(group)], group)
        own = [every[m][:width] for m in range(group)]
        here = at_seq // group
        ahead = {
            far: [
                lax.dynamic_slice_in_dim(
                    every[m], jnp.maximum((here ^ far) - here, 0) * width, width, 0
                )
                for m in range(group)
            ]
            for far in range(1, groups)
        }
    pieces = [own[0]]
    for m in range(1, group):
        pieces.append(swap(own[m], "seq", m))
    for far in range(1, groups):
        for m in range(group):
            pieces.append(swap(ahead[far][m], "seq", far * group + m))
    return finish(pieces, group)


def solution(mesh):
    in_specs = (P("seq", "chan"), P(None, None, "chan"), P(None, "seq"))
    out_specs = P("seq", "chan")
    return jax.shard_map(local, mesh=mesh, in_specs=in_specs, out_specs=out_specs, check_vma=False)
```

```python
import jax
import jax.numpy as jnp
from jax import lax
from jax.experimental import pallas as pl
from jax.experimental.pallas import tpu as pltpu
from jax.sharding import PartitionSpec as P


f32 = jnp.float32
bf16 = jnp.bfloat16
LANES = 128


def swap(value, axis, mask):
    return lax.ppermute(value, axis, [(i, i ^ mask) for i in range(lax.axis_size(axis))])


def params(mib, axes=1):
    return pltpu.CompilerParams(
        dimension_semantics=("arbitrary",) * axes if axes else None,
        vmem_limit_bytes=mib * 1024 * 1024,
    )


def on_device(body, group, **settings):
    def kernel(*refs):
        seq = lax.axis_index("seq")
        place, own = seq & (group - 1), lax.shift_right_logical(seq, group.bit_length() - 1)
        body((lax.axis_index("chan"), place, own, seq), *refs, group=group, **settings)

    return kernel


def columns_of(w, place, group, targets):
    sub = w.shape[1] // group
    return jnp.concatenate(
        [w[:, pl.ds(pl.multiple_of((place ^ m) * sub, sub), sub)] for m in targets], axis=1
    )


def project_first_body(meta, mine_ref, w_ref, *refs, group, targets):
    sum_refs, (ahead_ref, mine, held, sems, sem) = refs[:-5], refs[-5:]
    depth = mine_ref.shape[1]
    count = w_ref.shape[0]
    own = pltpu.make_async_copy(mine_ref, mine, sem)
    own.start()

    def fetch(m, k):
        rows = pl.ds(pl.multiple_of((meta[0] ^ m) * depth, depth), depth)
        target = ahead_ref.at[m - 1, k] if m else held.at[k]
        return pltpu.make_async_copy(w_ref.at[k, rows, :], target, sems.at[m, k])

    copies = [[fetch(m, k) for k in range(count)] for m in range(sems.shape[0])]
    for copy in copies[0]:
        copy.start()
    own.wait()
    for k in range(count):
        copies[0][k].wait()
        if k == 0:
            for copy in [copy for later in copies[1:] for copy in later]:
                copy.start()
        for sum_ref, places in zip(sum_refs, targets, strict=True):
            sum_ref[k] = jnp.dot(
                mine[...],
                columns_of(held.at[k], meta[1], group, places),
                preferred_element_type=f32,
            )
    for copy in [copy for later in copies[1:] for copy in later]:
        copy.wait()


def project_first(mine, weights, chan, group, targets):
    tokens, depth = mine.shape
    count, _, width = weights.shape
    sub = width // group
    vmem, hbm = pl.BlockSpec(memory_space=pltpu.VMEM), pl.BlockSpec(memory_space=pltpu.HBM)
    return pl.pallas_call(
        on_device(project_first_body, group=group, targets=targets),
        in_specs=[hbm, hbm],
        out_specs=[vmem] * (len(targets) + 1),
        scratch_shapes=[
            pltpu.VMEM((tokens, depth), bf16),
            pltpu.VMEM((count, depth, width), bf16),
            pltpu.SemaphoreType.DMA((chan, count)),
            pltpu.SemaphoreType.DMA,
        ],
        out_shape=[
            jax.ShapeDtypeStruct((count, tokens, len(places) * sub), f32) for places in targets
        ]
        + [jax.ShapeDtypeStruct((chan - 1, count, depth, width), bf16)],
        compiler_params=params(32, 0),
        cost_estimate=pl.CostEstimate(
            flops=2 * tokens * depth * width * count,
            bytes_accessed=2 * weights.size,
            transcendentals=0,
        ),
        name="project_first",
    )(pltpu.with_memory_space_constraint(mine, pltpu.HBM), weights)


def project_body(meta, *refs, blocks, group, places, last, riders):
    x_refs, (w_ref, before_ref) = refs[: len(blocks)], refs[len(blocks) : len(blocks) + 2]
    out_refs = refs[len(blocks) + 2 :]
    count, tokens, _ = before_ref.shape
    sub = w_ref.shape[3] // group
    if riders:
        pieces_ref, out_refs = out_refs[0], out_refs[1:]
        pieces = jnp.concatenate([pieces_ref[i] for i in range(pieces_ref.shape[0])])
        for out_ref in out_refs:
            out_ref[tokens:, :] = jnp.zeros((pieces.shape[0], out_ref.shape[1]), bf16)
            out_ref[tokens:, 0 : pieces.shape[1]] = pieces.astype(bf16)
    x = jnp.concatenate([x_ref[...] for x_ref in x_refs], axis=1)
    for k in range(count):
        rows = [columns_of(w_ref.at[m - 1, k], meta[1], group, places) for m in blocks]
        total = before_ref[k] + jnp.dot(
            x, jnp.concatenate(rows, axis=0), preferred_element_type=f32
        )
        if last:
            for i, out_ref in enumerate(out_refs):
                out_ref[0:tokens, k * sub : (k + 1) * sub] = total[
                    :, i * sub : (i + 1) * sub
                ].astype(bf16)
        else:
            out_refs[0][k] = total


def project(held, blocks, ahead, before, group, places, last, riders):
    count, tokens, columns = before.shape
    depth = ahead.shape[2]
    width = count * columns // len(places)
    vmem = pl.BlockSpec(memory_space=pltpu.VMEM)
    extra = 0 if riders is None else riders.shape[0] * riders.shape[1]
    if last:
        out_shape = [
            jax.ShapeDtypeStruct((tokens + extra, width), bf16) for _ in places
        ]
    else:
        out_shape = [jax.ShapeDtypeStruct(before.shape, f32)]
    args = [held[m] for m in blocks] + [ahead, before] + ([] if riders is None else [riders])
    return pl.pallas_call(
        on_device(project_body, blocks=blocks,
            group=group,
            places=places,
            last=last,
            riders=riders is not None,
        ),
        in_specs=[vmem] * len(args),
        out_specs=[vmem] * len(out_shape),
        out_shape=out_shape,
        compiler_params=params(32, 0),
        cost_estimate=pl.CostEstimate(
            flops=2 * tokens * depth * len(blocks) * columns * count,
            bytes_accessed=2 * depth * len(blocks) * columns * count,
            transcendentals=0,
        ),
    )(*args)


def toeplitz_body(meta, *refs, order, group):
    (pieces_ref, far_ref), rider_refs, (out_ref, row) = refs[:2], refs[2:-2], refs[-2:]
    count, width = pieces_ref.shape[1:]
    slices = pieces_ref.shape[0]
    tokens = rider_refs[0].shape[0] - slices * count
    length = len(order) * width
    step = pl.program_id(0)

    @pl.when(step == 0)
    def _():
        row[:, pl.ds(length, width)] = jnp.zeros((row.shape[0], width), f32)
        across = lax.broadcasted_iota(jnp.int32, (width, width), 0)
        along = lax.broadcasted_iota(jnp.int32, (width, width), 1)
        mirror = (across + along == width - 1).astype(bf16)
        near, far = [
            jnp.concatenate([ref[i] for i in range(slices)]).astype(bf16)
            for ref in (pieces_ref, far_ref)
        ]
        riders = [ref[tokens:, 0:width] for ref in rider_refs]
        pieces = jnp.concatenate([near, *riders, far])
        turned = jnp.dot(pieces, mirror, preferred_element_type=f32)
        for at, m in enumerate(order):
            start = length - width * ((meta[3] ^ m) + 1)
            row[0:count, pl.ds(pl.multiple_of(start, width), width)] = turned[
                at * count : (at + 1) * count
            ]

    span = group * width

    @pl.when(step == 0)
    def _():
        out_ref[...] = jnp.zeros(out_ref.shape, bf16)

    @pl.when(step > 0)
    def _():
        start = pl.multiple_of(length - span * step, width)
        for k in range(count):
            line = jnp.broadcast_to(
                row[k : k + 1, pl.ds(start, span + width)], (LANES, span + width)
            )
            turned = pltpu.roll(line, 1, 1, stride=1, stride_axis=0).astype(bf16)
            for e in range(group):
                for h in range(width // LANES):
                    at = span - width * e - LANES * h
                    out_ref[
                        e * width + h * LANES : e * width + (h + 1) * LANES,
                        k * width : (k + 1) * width,
                    ] = turned[:, at : at + width]


def toeplitz(pieces, far, riders, order, group):
    _, count, width = pieces.shape
    blocks = len(order)
    rows, columns = group * width, count * width
    return pl.pallas_call(
        on_device(toeplitz_body, order=order, group=group),
        grid_spec=pltpu.PrefetchScalarGridSpec(
            num_scalar_prefetch=0,
            grid=(blocks // group + 1,),
            in_specs=[pl.BlockSpec(memory_space=pltpu.VMEM)] * (2 + len(riders)),
            out_specs=pl.BlockSpec((rows, columns), lambda i: (i, 0)),
            scratch_shapes=[pltpu.VMEM((8, (blocks + 1) * width), f32)],
        ),
        out_shape=jax.ShapeDtypeStruct(((blocks + group) * width, columns), bf16),
        compiler_params=params(16),
        cost_estimate=pl.CostEstimate(
            flops=blocks * width * columns * 8,
            bytes_accessed=2 * blocks * width * columns,
            transcendentals=0,
        ),
        name="toeplitz",
    )(pieces, far, *riders)


def place_parts(held, p_refs, places, sub, width):
    for p_ref, place in zip(p_refs, places, strict=True):
        at = pl.multiple_of(place * sub, sub)
        for k in range(p_ref.shape[1] // sub):
            held[k * width : (k + 1) * width, pl.ds(at, sub)] = p_ref[0:width, k * sub : (k + 1) * sub]


def pair_sums(rows, group, width, sub):
    return [
        rows[(r + 1) * width : (r + 2) * width, :sub] + rows[r * width : (r + 1) * width, sub:]
        for r in range(group)
    ]


def store_parts(out_refs, placed, sums, place):
    for r, value in enumerate(sums):
        placed[place ^ r] = value.astype(bf16)
    for m, out_ref in enumerate(out_refs):
        out_ref[...] = placed[m]


def convolve_pair_body(meta, table_ref, *refs, at, ahead, group, sub, last):
    p_refs, refs = refs[:2], refs[2:]
    width = min(p_ref.shape[0] for p_ref in p_refs)
    if last:
        sum_refs, out_refs, (held, placed) = refs[:1], refs[1:-2], refs[-2:]
    else:
        sum_refs, out_refs, (held,) = (), refs[:-1], refs[-1:]
    place = meta[1]
    place_parts(held, p_refs, [place & 1, 1 - (place & 1)], sub, width)
    for i, far in enumerate(ahead):
        start = (far + 1) * group - 1 - 2 * ((place // 2) ^ at)
        rows = table_ref[pl.ds(pl.multiple_of(start * width, width), (group + 1) * width), :]
        sums = pair_sums(
            jnp.dot(rows, held[...], preferred_element_type=f32), group, width, sub
        )
        if last:
            sums = [value + sum_refs[0][r] for r, value in enumerate(sums)]
            store_parts(out_refs, placed, sums, place)
        else:
            for r, value in enumerate(sums):
                out_refs[i][r] = value


def convolve_pair(table, parts, before, at, ahead, group):
    width = min(part.shape[0] for part in parts)
    columns = table.shape[1]
    sub = parts[0].shape[1] * width // columns
    last = before is not None
    vmem = pl.BlockSpec(memory_space=pltpu.VMEM)
    if last:
        out_shape = [jax.ShapeDtypeStruct((width, sub), bf16)] * group
        scratch = [pltpu.VMEM((group, width, sub), bf16)]
    else:
        out_shape = [jax.ShapeDtypeStruct((group, width, sub), f32)] * len(ahead)
        scratch = []
    args = [table, *parts] + ([before] if last else [])
    return pl.pallas_call(
        on_device(convolve_pair_body, at=at, ahead=ahead, group=group, sub=sub, last=last
        ),
        in_specs=[vmem] * len(args),
        out_specs=[vmem] * len(out_shape),
        out_shape=out_shape,
        scratch_shapes=[pltpu.VMEM((columns, 2 * sub), bf16), *scratch],
        compiler_params=params(32, 0),
        cost_estimate=pl.CostEstimate(
            flops=4 * len(ahead) * (group + 1) * width * columns * sub,
            bytes_accessed=2 * width * columns,
            transcendentals=0,
        ),
    )(*args)


def convolve_one_body(meta, table_ref, p_ref, *refs, m, ahead, group, width, sub, last):
    count = len(ahead)
    sum_refs, refs = refs[:count], refs[count:]
    out_refs, (held, placed) = refs[:-2], refs[-2:]
    place = meta[1]
    for k in range(held.shape[0] // width):
        held[k * width : (k + 1) * width, :] = p_ref[0:width, k * sub : (k + 1) * sub]
    for i, far in enumerate(ahead):
        start = (far + 1) * group - (place ^ m)
        rows = table_ref[pl.ds(pl.multiple_of(start * width, width), group * width), :]
        value = jnp.dot(rows, held[...], preferred_element_type=f32)
        sums = [value[r * width : (r + 1) * width] + sum_refs[i][r] for r in range(group)]
        if last:
            store_parts(out_refs, placed, sums, place)
        else:
            for r, total in enumerate(sums):
                out_refs[i][r] = total


def convolve_one(table, part, befores, m, ahead, group, last):
    _, width, sub = befores[0].shape
    columns = table.shape[1]
    vmem = pl.BlockSpec(memory_space=pltpu.VMEM)
    if last:
        out_shape = [jax.ShapeDtypeStruct((width, sub), bf16)] * group
    else:
        out_shape = [jax.ShapeDtypeStruct(before.shape, f32) for before in befores]
    args = [table, part, *befores]
    return pl.pallas_call(
        on_device(
            convolve_one_body, m=m, ahead=ahead, group=group, width=width, sub=sub, last=last
        ),
        in_specs=[vmem] * len(args),
        out_specs=[vmem] * len(out_shape),
        out_shape=out_shape,
        scratch_shapes=[pltpu.VMEM((columns, sub), bf16), pltpu.VMEM((group, width, sub), bf16)],
        compiler_params=params(32, 0),
        cost_estimate=pl.CostEstimate(
            flops=2 * len(ahead) * group * width * columns * sub,
            bytes_accessed=2 * width * columns,
            transcendentals=0,
        ),
    )(*args)


def convolve_all_body(meta, low_ref, high_ref, *refs, group, sub):
    p_refs, out_refs, (held, placed) = refs[:group], refs[group : 2 * group], refs[2 * group :]
    width = p_refs[0].shape[0]

    @pl.when(pl.program_id(0) == 0)
    def _():
        place_parts(held, p_refs, [meta[1] ^ m for m in range(group)], sub, width)

    sums = None
    for at in range(0, group, 2):
        side = held[:, at * sub : (at + 2) * sub]
        split = (group - 1 - at) * width
        rows = jnp.concatenate(
            [
                jnp.dot(low_ref[split:, :], side, preferred_element_type=f32),
                jnp.dot(high_ref[: (group - at) * width, :], side, preferred_element_type=f32),
            ]
        )
        more = pair_sums(rows, group, width, sub)
        sums = more if sums is None else [a + b for a, b in zip(sums, more, strict=True)]
    store_parts(out_refs, placed, sums, meta[1])


def convolve_all(table, parts, group):
    width = parts[0].shape[0]
    columns = table.shape[1]
    sub = parts[0].shape[1] * width // columns
    rows = group * width
    steps = table.shape[0] // rows - 1
    return pl.pallas_call(
        on_device(convolve_all_body, group=group, sub=sub),
        grid_spec=pltpu.PrefetchScalarGridSpec(
            num_scalar_prefetch=0,
            grid=(steps,),
            in_specs=[
                pl.BlockSpec((rows, columns), lambda i: (i, 0)),
                pl.BlockSpec((rows, columns), lambda i: (i + 1, 0)),
            ]
            + [pl.BlockSpec(part.shape, lambda i: (0, 0)) for part in parts],
            out_specs=[pl.BlockSpec((width, sub), lambda i: (i, 0))] * group,
            scratch_shapes=[
                pltpu.VMEM((columns, group * sub), bf16),
                pltpu.VMEM((group, width, sub), bf16),
            ],
        ),
        out_shape=[jax.ShapeDtypeStruct((steps * width, sub), bf16)] * group,
        compiler_params=params(32),
        cost_estimate=pl.CostEstimate(
            flops=2 * steps * rows * columns * group * sub,
            bytes_accessed=2 * steps * rows * columns,
            transcendentals=0,
        ),
        name="convolve_all",
    )(table, table, *parts)


def finish_body(meta, *refs, group):
    parts, out_ref = refs[:-1], refs[-1]
    sub = out_ref.shape[1] // group
    place, own = meta[1], meta[2]
    for m in range(group):
        value = parts[m][...].astype(f32)
        for far in range(1, len(parts) // group):
            other = parts[far * group + m][...].astype(f32)
            value = value + jnp.where((own ^ far) < own, other, 0.0)
        at = pl.multiple_of((place ^ m) * sub, sub)
        out_ref[:, pl.ds(at, sub)] = value.astype(bf16)


def finish(parts, group):
    width, sub = parts[0].shape
    shape = (width, sub * group)
    return pl.pallas_call(
        on_device(finish_body, group=group),
        in_specs=[pl.BlockSpec(memory_space=pltpu.VMEM)] * len(parts),
        out_specs=pl.BlockSpec(memory_space=pltpu.VMEM),
        out_shape=jax.ShapeDtypeStruct(shape, bf16),
        compiler_params=params(24, 0),
        name="finish",
    )(*parts)


def local(inputs, weights, filters):
    seq, chan = lax.axis_size("seq"), lax.axis_size("chan")
    group = min(4, seq)
    groups = seq // group
    width = inputs.shape[0]
    at_seq = lax.axis_index("seq")
    held = {0: inputs}
    held[2] = swap(inputs, "chan", 2)
    held[1] = swap(inputs, "chan", 1)
    held[3] = swap(held[2], "chan", 1)

    weights = pltpu.with_memory_space_constraint(weights, pltpu.HBM)
    pieces = filters[None]
    order = [0]
    bit = seq // 2
    while bit >= group:
        pieces = jnp.concatenate([pieces, swap(pieces, "seq", bit)])
        order += [m ^ bit for m in order]
        bit //= 2
    order = [m ^ near for near in range(group) for m in order]

    soon = [m for m in range(1, group) if m < 3]
    late = [m for m in range(group) if m not in soon]
    to_soon, to_late, ahead = project_first(inputs, weights, chan, group, [soon, late])
    (to_soon,) = project(held, [1, 2], ahead, to_soon, group, soon, False, None)
    mine = project(held, [3], ahead, to_soon, group, soon, True, pieces)
    mine += project(held, [1, 2, 3], ahead, to_late, group, late, True, None)
    mine = dict(zip(soon + late, mine, strict=True))
    parts = {0: mine[0]}
    for m in range(1, group):
        parts[m] = swap(mine[m], "seq", m)
    parts = [parts[m] for m in range(group)]
    far_pieces = swap(pieces, "seq", 3)
    table = toeplitz(pieces, far_pieces, parts[1:3], order, group)

    if groups == 2 and group == 4:
        sums = convolve_pair(table, parts[:2], None, 0, (0, 1), group)
        own, after = convolve_one(table, parts[2], sums, 2, (0, 1), group, False)
        after = convolve_one(table, parts[3], [after], 3, (1,), group, True)
        own = convolve_one(table, parts[3], [own], 3, (0,), group, True)
        ahead = {1: after}
    else:
        every = convolve_all(table, [parts[m] for m in range(group)], group)
        own = [every[m][:width] for m in range(group)]
        here = at_seq // group
        ahead = {
            far: [
                lax.dynamic_slice_in_dim(
                    every[m], jnp.maximum((here ^ far) - here, 0) * width, width, 0
                )
                for m in range(group)
            ]
            for far in range(1, groups)
        }
    pieces = [own[0]]
    for m in range(1, group):
        pieces.append(swap(own[m], "seq", m))
    for far in range(1, groups):
        for m in range(group):
            pieces.append(swap(ahead[far][m], "seq", far * group + m))
    return finish(pieces, group)


def solution(mesh):
    in_specs = (P("seq", "chan"), P(None, None, "chan"), P(None, "seq"))
    out_specs = P("seq", "chan")
    return jax.shard_map(local, mesh=mesh, in_specs=in_specs, out_specs=out_specs, check_vma=False)
```

```python
import jax
import jax.numpy as jnp
from jax import lax
from jax.experimental import pallas as pl
from jax.experimental.pallas import tpu as pltpu
from jax.sharding import PartitionSpec as P


f32 = jnp.float32
bf16 = jnp.bfloat16
LANES = 128


def swap(value, axis, mask):
    return lax.ppermute(value, axis, [(i, i ^ mask) for i in range(lax.axis_size(axis))])


def params(mib, axes=1):
    return pltpu.CompilerParams(
        dimension_semantics=("arbitrary",) * axes if axes else None,
        vmem_limit_bytes=mib * 1024 * 1024,
    )


def on_device(body, group, **settings):
    def kernel(*refs):
        seq = lax.axis_index("seq")
        place, own = seq & (group - 1), lax.shift_right_logical(seq, group.bit_length() - 1)
        body((lax.axis_index("chan"), place, own, seq), *refs, group=group, **settings)

    return kernel


def columns_of(w, place, group, targets):
    sub = w.shape[1] // group
    return jnp.concatenate(
        [w[:, pl.ds(pl.multiple_of((place ^ m) * sub, sub), sub)] for m in targets], axis=1
    )


def project_first_body(meta, mine_ref, w_ref, *refs, group, targets):
    sum_refs, (ahead_ref, mine, held, sems, sem) = refs[:-5], refs[-5:]
    depth = mine_ref.shape[1]
    count = w_ref.shape[0]
    own = pltpu.make_async_copy(mine_ref, mine, sem)
    own.start()

    def fetch(m, k):
        rows = pl.ds(pl.multiple_of((meta[0] ^ m) * depth, depth), depth)
        target = ahead_ref.at[m - 1, k] if m else held.at[k]
        return pltpu.make_async_copy(w_ref.at[k, rows, :], target, sems.at[m, k])

    copies = [[fetch(m, k) for k in range(count)] for m in range(sems.shape[0])]
    for copy in copies[0]:
        copy.start()
    own.wait()
    for k in range(count):
        copies[0][k].wait()
        if k == 0:
            for copy in [copy for later in copies[1:] for copy in later]:
                copy.start()
        for sum_ref, places in zip(sum_refs, targets, strict=True):
            sum_ref[k] = jnp.dot(
                mine[...],
                columns_of(held.at[k], meta[1], group, places),
                preferred_element_type=f32,
            )
    for copy in [copy for later in copies[1:] for copy in later]:
        copy.wait()


def project_first(mine, weights, chan, group, targets):
    tokens, depth = mine.shape
    count, _, width = weights.shape
    sub = width // group
    vmem, hbm = pl.BlockSpec(memory_space=pltpu.VMEM), pl.BlockSpec(memory_space=pltpu.HBM)
    return pl.pallas_call(
        on_device(project_first_body, group=group, targets=targets),
        in_specs=[hbm, hbm],
        out_specs=[vmem] * (len(targets) + 1),
        scratch_shapes=[
            pltpu.VMEM((tokens, depth), bf16),
            pltpu.VMEM((count, depth, width), bf16),
            pltpu.SemaphoreType.DMA((chan, count)),
            pltpu.SemaphoreType.DMA,
        ],
        out_shape=[
            jax.ShapeDtypeStruct((count, tokens, len(places) * sub), f32) for places in targets
        ]
        + [jax.ShapeDtypeStruct((chan - 1, count, depth, width), bf16)],
        compiler_params=params(32, 0),
        cost_estimate=pl.CostEstimate(
            flops=2 * tokens * depth * width * count,
            bytes_accessed=2 * weights.size,
            transcendentals=0,
        ),
        name="project_first",
    )(pltpu.with_memory_space_constraint(mine, pltpu.HBM), weights)


def project_body(meta, *refs, blocks, group, places, last, riders):
    x_refs, (w_ref, before_ref) = refs[: len(blocks)], refs[len(blocks) : len(blocks) + 2]
    out_refs = refs[len(blocks) + 2 :]
    count, tokens, _ = before_ref.shape
    sub = w_ref.shape[3] // group
    if riders:
        pieces_ref, out_refs = out_refs[0], out_refs[1:]
        pieces = jnp.concatenate([pieces_ref[i] for i in range(pieces_ref.shape[0])])
        for out_ref in out_refs:
            out_ref[tokens:, :] = jnp.zeros((pieces.shape[0], out_ref.shape[1]), bf16)
            out_ref[tokens:, 0 : pieces.shape[1]] = pieces.astype(bf16)
    x = jnp.concatenate([x_ref[...] for x_ref in x_refs], axis=1)
    for k in range(count):
        rows = [columns_of(w_ref.at[m - 1, k], meta[1], group, places) for m in blocks]
        total = before_ref[k] + jnp.dot(
            x, jnp.concatenate(rows, axis=0), preferred_element_type=f32
        )
        if last:
            for i, out_ref in enumerate(out_refs):
                out_ref[0:tokens, k * sub : (k + 1) * sub] = total[
                    :, i * sub : (i + 1) * sub
                ].astype(bf16)
        else:
            out_refs[0][k] = total


def project(held, blocks, ahead, before, group, places, last, riders):
    count, tokens, columns = before.shape
    depth = ahead.shape[2]
    width = count * columns // len(places)
    vmem = pl.BlockSpec(memory_space=pltpu.VMEM)
    extra = 0 if riders is None else riders.shape[0] * riders.shape[1]
    if last:
        out_shape = [
            jax.ShapeDtypeStruct((tokens + extra, width), bf16) for _ in places
        ]
    else:
        out_shape = [jax.ShapeDtypeStruct(before.shape, f32)]
    args = [held[m] for m in blocks] + [ahead, before] + ([] if riders is None else [riders])
    return pl.pallas_call(
        on_device(project_body, blocks=blocks,
            group=group,
            places=places,
            last=last,
            riders=riders is not None,
        ),
        in_specs=[vmem] * len(args),
        out_specs=[vmem] * len(out_shape),
        out_shape=out_shape,
        compiler_params=params(32, 0),
        cost_estimate=pl.CostEstimate(
            flops=2 * tokens * depth * len(blocks) * columns * count,
            bytes_accessed=2 * depth * len(blocks) * columns * count,
            transcendentals=0,
        ),
    )(*args)


def toeplitz_body(meta, *refs, order, group):
    (pieces_ref, far_ref), rider_refs, (out_ref, row) = refs[:2], refs[2:-2], refs[-2:]
    count, width = pieces_ref.shape[1:]
    slices = pieces_ref.shape[0]
    tokens = rider_refs[0].shape[0] - slices * count
    length = len(order) * width
    step = pl.program_id(0)

    @pl.when(step == 0)
    def _():
        row[:, pl.ds(length, width)] = jnp.zeros((row.shape[0], width), f32)
        across = lax.broadcasted_iota(jnp.int32, (width, width), 0)
        along = lax.broadcasted_iota(jnp.int32, (width, width), 1)
        mirror = (across + along == width - 1).astype(bf16)
        near, far = [
            jnp.concatenate([ref[i] for i in range(slices)]).astype(bf16)
            for ref in (pieces_ref, far_ref)
        ]
        riders = [ref[tokens:, 0:width] for ref in rider_refs]
        pieces = jnp.concatenate([near, *riders, far])
        turned = jnp.dot(pieces, mirror, preferred_element_type=f32)
        for at, m in enumerate(order):
            start = length - width * ((meta[3] ^ m) + 1)
            row[0:count, pl.ds(pl.multiple_of(start, width), width)] = turned[
                at * count : (at + 1) * count
            ]

    span = group * width

    @pl.when(step == 0)
    def _():
        out_ref[...] = jnp.zeros(out_ref.shape, bf16)

    @pl.when(step > 0)
    def _():
        start = pl.multiple_of(length - span * step, width)
        for k in range(count):
            line = jnp.broadcast_to(
                row[k : k + 1, pl.ds(start, span + width)], (LANES, span + width)
            )
            turned = pltpu.roll(line, 1, 1, stride=1, stride_axis=0).astype(bf16)
            for e in range(group):
                for h in range(width // LANES):
                    at = span - width * e - LANES * h
                    out_ref[
                        e * width + h * LANES : e * width + (h + 1) * LANES,
                        k * width : (k + 1) * width,
                    ] = turned[:, at : at + width]


def toeplitz(pieces, far, riders, order, group):
    _, count, width = pieces.shape
    blocks = len(order)
    rows, columns = group * width, count * width
    return pl.pallas_call(
        on_device(toeplitz_body, order=order, group=group),
        grid_spec=pltpu.PrefetchScalarGridSpec(
            num_scalar_prefetch=0,
            grid=(blocks // group + 1,),
            in_specs=[pl.BlockSpec(memory_space=pltpu.VMEM)] * (2 + len(riders)),
            out_specs=pl.BlockSpec((rows, columns), lambda i: (i, 0)),
            scratch_shapes=[pltpu.VMEM((8, (blocks + 1) * width), f32)],
        ),
        out_shape=jax.ShapeDtypeStruct(((blocks + group) * width, columns), bf16),
        compiler_params=params(16),
        cost_estimate=pl.CostEstimate(
            flops=blocks * width * columns * 8,
            bytes_accessed=2 * blocks * width * columns,
            transcendentals=0,
        ),
        name="toeplitz",
    )(pieces, far, *riders)


def place_parts(held, p_refs, places, sub, width):
    for p_ref, place in zip(p_refs, places, strict=True):
        at = pl.multiple_of(place * sub, sub)
        for k in range(p_ref.shape[1] // sub):
            held[k * width : (k + 1) * width, pl.ds(at, sub)] = p_ref[0:width, k * sub : (k + 1) * sub]


def pair_sums(rows, group, width, sub):
    return [
        rows[(r + 1) * width : (r + 2) * width, :sub] + rows[r * width : (r + 1) * width, sub:]
        for r in range(group)
    ]


def store_parts(out_refs, placed, sums, place):
    for r, value in enumerate(sums):
        placed[place ^ r] = value.astype(bf16)
    for m, out_ref in enumerate(out_refs):
        out_ref[...] = placed[m]


def convolve_pair_body(meta, table_ref, *refs, at, ahead, group, sub, last):
    p_refs, refs = refs[:2], refs[2:]
    width = min(p_ref.shape[0] for p_ref in p_refs)
    if last:
        sum_refs, out_refs, (held, placed) = refs[:1], refs[1:-2], refs[-2:]
    else:
        sum_refs, out_refs, (held,) = (), refs[:-1], refs[-1:]
    place = meta[1]
    place_parts(held, p_refs, [place & 1, 1 - (place & 1)], sub, width)
    for i, far in enumerate(ahead):
        start = (far + 1) * group - 1 - 2 * ((place // 2) ^ at)
        rows = table_ref[pl.ds(pl.multiple_of(start * width, width), (group + 1) * width), :]
        sums = pair_sums(
            jnp.dot(rows, held[...], preferred_element_type=f32), group, width, sub
        )
        if last:
            sums = [value + sum_refs[0][r] for r, value in enumerate(sums)]
            store_parts(out_refs, placed, sums, place)
        else:
            for r, value in enumerate(sums):
                out_refs[i][r] = value


def convolve_pair(table, parts, before, at, ahead, group):
    width = min(part.shape[0] for part in parts)
    columns = table.shape[1]
    sub = parts[0].shape[1] * width // columns
    last = before is not None
    vmem = pl.BlockSpec(memory_space=pltpu.VMEM)
    if last:
        out_shape = [jax.ShapeDtypeStruct((width, sub), bf16)] * group
        scratch = [pltpu.VMEM((group, width, sub), bf16)]
    else:
        out_shape = [jax.ShapeDtypeStruct((group, width, sub), f32)] * len(ahead)
        scratch = []
    args = [table, *parts] + ([before] if last else [])
    return pl.pallas_call(
        on_device(convolve_pair_body, at=at, ahead=ahead, group=group, sub=sub, last=last
        ),
        in_specs=[vmem] * len(args),
        out_specs=[vmem] * len(out_shape),
        out_shape=out_shape,
        scratch_shapes=[pltpu.VMEM((columns, 2 * sub), bf16), *scratch],
        compiler_params=params(32, 0),
        cost_estimate=pl.CostEstimate(
            flops=4 * len(ahead) * (group + 1) * width * columns * sub,
            bytes_accessed=2 * width * columns,
            transcendentals=0,
        ),
    )(*args)


def convolve_one_body(meta, table_ref, p_ref, *refs, m, ahead, group, width, sub, last):
    count = len(ahead)
    sum_refs, refs = refs[:count], refs[count:]
    out_refs, (held, placed) = refs[:-2], refs[-2:]
    place = meta[1]
    for k in range(held.shape[0] // width):
        held[k * width : (k + 1) * width, :] = p_ref[0:width, k * sub : (k + 1) * sub]
    for i, far in enumerate(ahead):
        start = (far + 1) * group - (place ^ m)
        rows = table_ref[pl.ds(pl.multiple_of(start * width, width), group * width), :]
        value = jnp.dot(rows, held[...], preferred_element_type=f32)
        sums = [value[r * width : (r + 1) * width] + sum_refs[i][r] for r in range(group)]
        if last:
            store_parts(out_refs, placed, sums, place)
        else:
            for r, total in enumerate(sums):
                out_refs[i][r] = total


def convolve_one(table, part, befores, m, ahead, group, last):
    _, width, sub = befores[0].shape
    columns = table.shape[1]
    vmem = pl.BlockSpec(memory_space=pltpu.VMEM)
    if last:
        out_shape = [jax.ShapeDtypeStruct((width, sub), bf16)] * group
    else:
        out_shape = [jax.ShapeDtypeStruct(before.shape, f32) for before in befores]
    args = [table, part, *befores]
    return pl.pallas_call(
        on_device(
            convolve_one_body, m=m, ahead=ahead, group=group, width=width, sub=sub, last=last
        ),
        in_specs=[vmem] * len(args),
        out_specs=[vmem] * len(out_shape),
        out_shape=out_shape,
        scratch_shapes=[pltpu.VMEM((columns, sub), bf16), pltpu.VMEM((group, width, sub), bf16)],
        compiler_params=params(32, 0),
        cost_estimate=pl.CostEstimate(
            flops=2 * len(ahead) * group * width * columns * sub,
            bytes_accessed=2 * width * columns,
            transcendentals=0,
        ),
    )(*args)


def convolve_all_body(meta, low_ref, high_ref, *refs, group, sub):
    p_refs, out_refs, (held, placed) = refs[:group], refs[group : 2 * group], refs[2 * group :]
    width = p_refs[0].shape[0]

    @pl.when(pl.program_id(0) == 0)
    def _():
        place_parts(held, p_refs, [meta[1] ^ m for m in range(group)], sub, width)

    sums = None
    for at in range(0, group, 2):
        side = held[:, at * sub : (at + 2) * sub]
        split = (group - 1 - at) * width
        rows = jnp.concatenate(
            [
                jnp.dot(low_ref[split:, :], side, preferred_element_type=f32),
                jnp.dot(high_ref[: (group - at) * width, :], side, preferred_element_type=f32),
            ]
        )
        more = pair_sums(rows, group, width, sub)
        sums = more if sums is None else [a + b for a, b in zip(sums, more, strict=True)]
    store_parts(out_refs, placed, sums, meta[1])


def convolve_all(table, parts, group):
    width = parts[0].shape[0]
    columns = table.shape[1]
    sub = parts[0].shape[1] * width // columns
    rows = group * width
    steps = table.shape[0] // rows - 1
    return pl.pallas_call(
        on_device(convolve_all_body, group=group, sub=sub),
        grid_spec=pltpu.PrefetchScalarGridSpec(
            num_scalar_prefetch=0,
            grid=(steps,),
            in_specs=[
                pl.BlockSpec((rows, columns), lambda i: (i, 0)),
                pl.BlockSpec((rows, columns), lambda i: (i + 1, 0)),
            ]
            + [pl.BlockSpec(part.shape, lambda i: (0, 0)) for part in parts],
            out_specs=[pl.BlockSpec((width, sub), lambda i: (i, 0))] * group,
            scratch_shapes=[
                pltpu.VMEM((columns, group * sub), bf16),
                pltpu.VMEM((group, width, sub), bf16),
            ],
        ),
        out_shape=[jax.ShapeDtypeStruct((steps * width, sub), bf16)] * group,
        compiler_params=params(32),
        cost_estimate=pl.CostEstimate(
            flops=2 * steps * rows * columns * group * sub,
            bytes_accessed=2 * steps * rows * columns,
            transcendentals=0,
        ),
        name="convolve_all",
    )(table, table, *parts)


def finish_body(meta, *refs, group):
    parts, (out_ref, held, sems) = refs[:-3], refs[-3:]
    copies = []
    sub = out_ref.shape[1] // group
    place, own = meta[1], meta[2]
    for m in range(group):
        value = parts[m][...].astype(f32)
        for far in range(1, len(parts) // group):
            other = parts[far * group + m][...].astype(f32)
            value = value + jnp.where((own ^ far) < own, other, 0.0)
        at = pl.multiple_of((place ^ m) * sub, sub)
        held[m] = value.astype(bf16)
        copies.append(
            pltpu.make_async_copy(held.at[m], out_ref.at[:, pl.ds(at, sub)], sems.at[m])
        )
        copies[m].start()
    for copy in copies:
        copy.wait()


def finish(parts, group):
    width, sub = parts[0].shape
    shape = (width, sub * group)
    return pl.pallas_call(
        on_device(finish_body, group=group),
        in_specs=[pl.BlockSpec(memory_space=pltpu.VMEM)] * len(parts),
        out_specs=pl.BlockSpec(memory_space=pltpu.HBM),
        scratch_shapes=[
            pltpu.VMEM((group, width, sub), bf16),
            pltpu.SemaphoreType.DMA((group,)),
        ],
        out_shape=jax.ShapeDtypeStruct(shape, bf16),
        compiler_params=params(24, 0),
        name="finish",
    )(*parts)


def local(inputs, weights, filters):
    seq, chan = lax.axis_size("seq"), lax.axis_size("chan")
    group = min(4, seq)
    groups = seq // group
    width = inputs.shape[0]
    at_seq = lax.axis_index("seq")
    held = {0: inputs}
    held[2] = swap(inputs, "chan", 2)
    held[1] = swap(inputs, "chan", 1)
    held[3] = swap(held[2], "chan", 1)

    weights = pltpu.with_memory_space_constraint(weights, pltpu.HBM)
    pieces = filters[None]
    order = [0]
    bit = seq // 2
    while bit >= group:
        pieces = jnp.concatenate([pieces, swap(pieces, "seq", bit)])
        order += [m ^ bit for m in order]
        bit //= 2
    order = [m ^ near for near in range(group) for m in order]

    soon = [m for m in range(1, group) if m < 3]
    late = [m for m in range(group) if m not in soon]
    to_soon, to_late, ahead = project_first(inputs, weights, chan, group, [soon, late])
    (to_soon,) = project(held, [1, 2], ahead, to_soon, group, soon, False, None)
    mine = project(held, [3], ahead, to_soon, group, soon, True, pieces)
    mine += project(held, [1, 2, 3], ahead, to_late, group, late, True, None)
    mine = dict(zip(soon + late, mine, strict=True))
    parts = {0: mine[0]}
    for m in range(1, group):
        parts[m] = swap(mine[m], "seq", m)
    parts = [parts[m] for m in range(group)]
    far_pieces = swap(pieces, "seq", 3)
    table = toeplitz(pieces, far_pieces, parts[1:3], order, group)

    if groups == 2 and group == 4:
        sums = convolve_pair(table, parts[:2], None, 0, (0, 1), group)
        own, after = convolve_one(table, parts[2], sums, 2, (0, 1), group, False)
        after = convolve_one(table, parts[3], [after], 3, (1,), group, True)
        own = convolve_one(table, parts[3], [own], 3, (0,), group, True)
        ahead = {1: after}
    else:
        every = convolve_all(table, [parts[m] for m in range(group)], group)
        own = [every[m][:width] for m in range(group)]
        here = at_seq // group
        ahead = {
            far: [
                lax.dynamic_slice_in_dim(
                    every[m], jnp.maximum((here ^ far) - here, 0) * width, width, 0
                )
                for m in range(group)
            ]
            for far in range(1, groups)
        }
    pieces = [own[0]]
    for m in range(1, group):
        pieces.append(swap(own[m], "seq", m))
    for far in range(1, groups):
        for m in range(group):
            pieces.append(swap(ahead[far][m], "seq", far * group + m))
    return finish(pieces, group)


def solution(mesh):
    in_specs = (P("seq", "chan"), P(None, None, "chan"), P(None, "seq"))
    out_specs = P("seq", "chan")
    return jax.shard_map(local, mesh=mesh, in_specs=in_specs, out_specs=out_specs, check_vma=False)
```
